32 devices in a mesh: band: 4 (over x, core), grid: 8 (over z, y).
Axes of the slice: x: 2, y: 2, z: 4, core: 2. Of those that a mesh axis runs over, the one named last changes fastest.
Arguments:
- orbitals: float32 [8, 8, 8, 4, 16, 256], P('band', None, 'grid'), may hold values from -6 to 6
- potential: float32 [8, 4, 16, 256], P('grid'), may hold values from -1 to 0.5
- kinetic: float32 [3, 8, 4, 16, 256], P(None, 'grid'), may hold values from 0.5 to 1.5
- occupations: float32 [8, 8], P('band'), may hold values from 0.01 to 0.08
Outputs:
- filtered: float32 [8, 8, 8, 4, 16, 256], P('band', None, 'grid')
- gram: float32 [8, 8, 8], P('band')
- density: float32 [8, 4, 16, 256], P('grid', None, 'band')
The draws below stay inside these ranges and needn't reach their ends.
All inputs are finite; a program needn't handle non-finite values.
Results may differ from the reference program's by a relative error of at most 0.000052.
Values sent between devices are 32-bit elements; how exact they have to be, the bound alone decides.
No kernel may reach another device: no remote copies, remote signals or barrier semaphores. Data moves between devices by JAX's collectives and lax.ppermute only.
A program may use at most 64 MiB of HBM per device.

```python
import jax
import jax.numpy as jnp
from jax import lax

CX = 4
CY = 16
NZ = 256
BAND_BLK = 8
DEGREE = 4
PY = 8
PX = 1
DOMAINS = 8
NX = 4
NY = 128
BLOCKS = 8


def shard_levels(stream_key, dims, shards, low, largest):
    def one(position, parts):
        heights = jax.random.uniform(jax.random.fold_in(jax.random.fold_in(stream_key, 6), position), (parts,), jnp.float32, low / len(shards), largest / len(shards))
        return jnp.repeat(jnp.exp(heights), dims[position] // parts).reshape((-1,) + (1,) * (len(dims) - position - 1))

    factor_of = one(*shards[0])
    for cut in shards[1:]:
        factor_of = factor_of * one(*cut)
    return factor_of


def gaussian(key, dims, scale, most, cuts=(), held_as=jnp.bfloat16):
    drawn = jax.random.normal(key, dims, jnp.float32) * scale
    if len(cuts) > 0:
        drawn = shard_levels(key, dims, cuts, -0.22, 0.18) * drawn
    return jnp.clip(drawn, min=-most, max=most).astype(held_as)


def setup_inputs(seed: int = 0) -> dict:
    keys = jax.random.split(jax.random.key(seed), 5)
    orbitals = gaussian(keys[0], (BLOCKS, BAND_BLK, DOMAINS, CX, CY, NZ), 1.0, 6.0, ((0, 4), (2, 8)), jnp.float32)
    potential = jnp.clip(-1.0 + 1.5 * jax.random.uniform(keys[1], (DOMAINS, CX, CY, NZ), jnp.float32) ** shard_levels(keys[1], (DOMAINS, CX, CY, NZ), ((0, 8),), -0.2, 0.2), -1.0, 0.5)
    kinetic = jnp.clip(0.5 + 1.0 * jax.random.uniform(keys[2], (3, DOMAINS, CX, CY, NZ), jnp.float32) ** shard_levels(keys[2], (3, DOMAINS, CX, CY, NZ), ((1, 8),), -0.2, 0.2), 0.5, 1.5)
    occupations = jnp.clip(0.01 + 0.07 * jax.random.uniform(keys[3], (BLOCKS, BAND_BLK), jnp.float32) ** shard_levels(keys[3], (BLOCKS, BAND_BLK), ((0, 4),), -0.2, 0.2), 0.01, 0.08)
    return {"orbitals": orbitals, "potential": potential, "kinetic": kinetic, "occupations": occupations}


CENTRE = 6.0
HALF_WIDTH = 4.0
EPSILON = 1e-6


def assemble(field):
    lead = field.shape[:-4]
    count = len(lead)
    shaped = field.reshape(lead + (PX, PY, CX, CY, NZ))
    order = tuple(range(count)) + (count, count + 2, count + 1, count + 3, count + 4)
    shaped = jnp.transpose(shaped, order)
    return shaped.reshape(lead + (PX * CX, PY * CY, NZ))


def divide(field):
    lead = field.shape[:-3]
    count = len(lead)
    shaped = field.reshape(lead + (PX, CX, PY, CY, NZ))
    order = tuple(range(count)) + (count, count + 2, count + 1, count + 3, count + 4)
    shaped = jnp.transpose(shaped, order)
    return shaped.reshape(lead + (PX * PY, CX, CY, NZ))


def hamilton(field, potential, kinetic):
    total = jnp.zeros_like(field)
    for direction in range(3):
        axis_pos = direction - 3
        coeff = kinetic[direction]
        total = total + coeff * (field - jnp.roll(field, -1, axis_pos))
        total = total + jnp.roll(coeff, 1, axis_pos) * (field - jnp.roll(field, 1, axis_pos))
    return 0.5 * total + potential * field


def reference(orbitals, potential, kinetic, occupations):
    whole_pot = assemble(potential)
    whole_kin = assemble(kinetic)

    def filter_block(block):
        current = block
        previous = block
        for degree_step in range(DEGREE):
            image = hamilton(current, whole_pot, whole_kin)
            if degree_step == 0:
                fresh = (image - CENTRE * current) / HALF_WIDTH
            else:
                fresh = (2.0 / HALF_WIDTH) * (image - CENTRE * current) - previous
            previous = current
            current = fresh
        return current

    filtered = lax.map(filter_block, assemble(orbitals))
    cells = NX * NY * NZ
    flat = filtered.reshape(filtered.shape[0], filtered.shape[1], -1)
    gram = jnp.einsum("kbx,kcx->kbc", flat, flat, precision=lax.Precision.HIGHEST) / cells
    diagonal = jnp.diagonal(gram, axis1=1, axis2=2)
    weight = occupations / (diagonal + EPSILON)
    density = jnp.einsum("kb,kbxyz->xyz", weight, filtered * filtered, precision=lax.Precision.HIGHEST)
    return divide(filtered), gram, divide(density)
```

```python
import functools

import jax
import jax.numpy as jnp
from jax import lax
from jax.experimental import pallas as pl
from jax.experimental.pallas import tpu as pltpu
from jax.sharding import PartitionSpec as P

DEGREE = 4

CENTRE = 6.0
HALF_WIDTH = 4.0
EPSILON = 1e-06
SUB = 8
LANES = 128


def shifted(value, axis, steps):
    count = lax.axis_size(axis)
    pairs = [(source, (source + steps) % count) for source in range(count)]
    return lax.ppermute(value, axis, pairs)


def swapped(value, axis, bit):
    count = lax.axis_size(axis)
    return lax.ppermute(value, axis, [(i, i ^ bit) for i in range(count)])


def cut(h):
    return slice(LANES * h, LANES * (h + 1))


def iotas():
    return tuple(lax.broadcasted_iota(jnp.int32, (SUB, LANES), axis) for axis in range(2))


def ahead(line, lane):
    turned = [pltpu.roll(block, LANES - 1, 1) for block in line]
    return [jnp.where(lane == LANES - 1, turned[(h + 1) % len(line)], turned[h]) for h in range(len(line))]


def behind(line, lane):
    turned = [pltpu.roll(block, 1, 1) for block in line]
    return [jnp.where(lane == 0, turned[h - 1], turned[h]) for h in range(len(line))]


def pack_kernel(steps, odd_ref, pot_any, kin_any, orb_any, *refs):
    arrivals = refs[-1]
    pot_ref, kin_ref, orb_ref = refs[-4:-1]
    out_refs = refs[:-4]
    count, rows_x, rows_y, depth = orb_ref.shape
    odd = odd_ref[0] == 1
    row, _ = iotas()
    upper = row < DEGREE
    loads = [
        pltpu.make_async_copy(pot_any, pot_ref, arrivals.at[0]),
        pltpu.make_async_copy(kin_any, kin_ref, arrivals.at[1]),
    ]
    size = count // steps
    for k in range(steps):
        part = pl.ds(k * size, size)
        loads.append(pltpu.make_async_copy(orb_any.at[part], orb_ref.at[part], arrivals.at[2 + k]))
    for load in loads:
        load.start()
    fields = [pot_ref] + [kin_ref.at[c] for c in range(3)] + [orb_ref.at[m] for m in range(count)]
    place = 0
    for index in range(0, len(out_refs), 2):
        a_ref, b_ref = out_refs[index : index + 2]
        if index == 0:
            loads[0].wait()
            loads[1].wait()
        loads[2 + index // 2].wait()
        for p in range(a_ref.shape[0]):
            one, two = fields[place], fields[place + 1]
            place += 2
            for x in range(rows_x):
                for h in range(depth // LANES):
                    first = jnp.where(upper, one[x, 0:SUB, cut(h)], pltpu.roll(two[x, 0:SUB, cut(h)], DEGREE, 0))
                    tail = slice(rows_y - SUB, rows_y)
                    last = jnp.where(upper, pltpu.roll(one[x, tail, cut(h)], DEGREE, 0), two[x, tail, cut(h)])
                    a_ref[p, x, :, cut(h)] = jnp.where(odd, first, last)
                    b_ref[p, x, :, cut(h)] = jnp.where(odd, last, first)


def ring_tiles(ref, index, parts):
    return [
        [ref[index + (h, pl.ds(t, SUB, stride=parts), slice(None))] for h in range(ref.shape[-3])]
        for t in range(parts)
    ]


def own_coefficients(pot_ref, kin_ref, coef_ref, ring, lane):
    rows_x, rows_y, depth = pot_ref.shape
    parts = rows_y // SUB
    unit = 1.0 / HALF_WIDTH
    for x in range(rows_x):
        for c in range(4):
            own_ref = pot_ref if c == 0 else kin_ref.at[c - 1]
            for h in range(depth // LANES):
                ring[c, x, h] = own_ref[x, :, cut(h)]
    for x in range(rows_x):
        before = (x - 1) % rows_x
        pot = ring_tiles(ring, (0, x), parts)
        kx = ring_tiles(ring, (1, x), parts)
        kxm = ring_tiles(ring, (1, before), parts)
        ky = ring_tiles(ring, (2, x), parts)
        kz = ring_tiles(ring, (3, x), parts)
        for t in range(parts):
            kzm = behind(kz[t], lane)
            for h in range(depth // LANES):
                kym = ky[t - 1][h] if t > 0 else pltpu.roll(ky[parts - 1][h], 1, 0)
                total = kx[t][h] + kxm[t][h] + ky[t][h] + kym + kz[t][h] + kzm[h]
                coef_ref[0, x, t, h] = unit * total + (2.0 * unit) * (pot[t][h] - CENTRE)
                coef_ref[1, x, t, h] = unit * kx[t][h]
                coef_ref[2, x, t, h] = unit * ky[t][h]
                coef_ref[3, x, t, h] = unit * kz[t][h]
                coef_ref[4, x, t, h] = unit * kzm[h]
                if t == 0:
                    coef_ref[5, x, 0, h] = unit * kym


def apply_own(coef_ref, v, x, t, lane):
    rows_x, parts = len(v), len(v[0])
    up_x, down_x = (x + 1) % rows_x, (x - 1) % rows_x
    own = v[x][t]
    front, back = ahead(own, lane), behind(own, lane)
    result = []
    for h in range(len(own)):
        total = coef_ref[0, x, t, h] * own[h]
        total = total - coef_ref[1, x, t, h] * v[up_x][t][h]
        total = total - coef_ref[1, down_x, t, h] * v[down_x][t][h]
        above = v[x][t + 1][h] if t < parts - 1 else pltpu.roll(v[x][0][h], SUB - 1, 0)
        total = total - coef_ref[2, x, t, h] * above
        if t > 0:
            total = total - coef_ref[2, x, t - 1, h] * v[x][t - 1][h]
        else:
            total = total - coef_ref[5, x, 0, h] * pltpu.roll(v[x][parts - 1][h], 1, 0)
        total = total - coef_ref[3, x, t, h] * front[h]
        result.append(total - coef_ref[4, x, t, h] * back[h])
    return result


def pairs_of(members):
    return [(a, b) for a in range(members) for b in range(a, members)]


def interior_kernel(members, pot_ref, kin_ref, orb_ref, body_ref, seam_ref, sums_ref, coef_ref, coef_ring, ring):
    count, rows_x, rows_y, depth = orb_ref.shape
    parts = rows_y // SUB
    blocks_z = depth // LANES
    row, lane = iotas()
    upper = row < DEGREE
    own_coefficients(pot_ref, kin_ref, coef_ref, coef_ring, lane)

    def one(pair, half):
        m = 2 * pair + half
        for x in range(rows_x):
            for h in range(blocks_z):
                ring[half, x, h] = orb_ref[m, x, :, cut(h)]
        v = [ring_tiles(ring.at[half], (x,), parts) for x in range(rows_x)]
        previous = None
        for step in range(DEGREE):
            for x in range(rows_x):
                for h in range(blocks_z):
                    for side in range(2):
                        for depth_in in range(2):
                            y = step + depth_in if side == 0 else rows_y - 1 - step - depth_in
                            place = DEGREE * half + (DEGREE - 1 if side == 0 else 0)
                            value = v[x][y % parts][h][y // parts : y // parts + 1]
                            seam_ref[pair, side, step, depth_in, x, h, place : place + 1, :] = value
            fresh = []
            for x in range(rows_x):
                rows = []
                for t in range(parts):
                    image = apply_own(coef_ref, v, x, t, lane)
                    if step == 0:
                        rows.append([0.5 * i for i in image])
                    else:
                        rows.append([i - p for i, p in zip(image, previous[x][t])])
                fresh.append(rows)
            previous, v = v, fresh
        for x in range(rows_x):
            for t in range(parts):
                for h in range(blocks_z):
                    ring[half, x, h, pl.ds(t, SUB, stride=parts), :] = v[x][t][h]
        for x in range(rows_x):
            for h in range(blocks_z):
                body_ref[m, x, h] = jnp.where(upper, ring[half, x, h, rows_y - SUB :], ring[half, x, h, 0:SUB])

    def both(pair, carry):
        one(pair, 0)
        one(pair, 1)
        return carry

    lax.fori_loop(0, count // 2, both, 0)

    pairs = pairs_of(members)
    for k in range(count // members):

        def gather(x, sums, k=k):
            sums = list(sums)
            for h in range(blocks_z):
                f = [body_ref[k * members + a, x, h] for a in range(members)]
                for i, (a, b) in enumerate(pairs):
                    sums[i] = sums[i] + f[a] * f[b]
            return tuple(sums)

        sums = lax.fori_loop(0, rows_x, gather, tuple(jnp.zeros((SUB, LANES), jnp.float32) for _ in pairs))
        for i, value in enumerate(sums):
            sums_ref[k, i] = value


def windows_kernel(odd_ref, pot_ref, kin_ref, ha_ref, hb_ref, coef_ref):
    rows_x, rows_y, depth = pot_ref.shape
    odd = odd_ref[0] == 1
    row, lane = iotas()
    upper = row < DEGREE
    blocks_z = depth // LANES
    unit = 1.0 / HALF_WIDTH

    def window(tile, start):
        low = pltpu.roll(tile, (SUB - start) % SUB, 0) if start % SUB else tile
        high = pltpu.roll(tile, (SUB + DEGREE - start) % SUB, 0) if (DEGREE - start) % SUB else tile
        return jnp.where(upper, low, high)

    def field(c, x, h):
        own_ref = pot_ref if c == 0 else kin_ref.at[c - 1]
        a, b = ha_ref[c // 2, x, :, cut(h)], hb_ref[c // 2, x, :, cut(h)]
        before, after = jnp.where(odd, a, b), jnp.where(odd, b, a)
        head, tail = own_ref[x, 0:SUB, cut(h)], own_ref[x, rows_y - SUB :, cut(h)]
        if c % 2:
            before = pltpu.roll(before, DEGREE, 0)
        top = jnp.where(upper, before, pltpu.roll(head, DEGREE, 0))
        if c % 2:
            after = pltpu.roll(after, DEGREE, 0)
        kept = pltpu.roll(tail, SUB - (DEGREE - 1), 0)
        bottom = jnp.where(row < DEGREE + 1, kept, pltpu.roll(after, DEGREE + 1, 0))
        return top, bottom

    for x in range(rows_x):
        before_x = (x - 1) % rows_x
        tiles = [[field(c, x, h) for h in range(blocks_z)] for c in range(4)]
        kxm = [field(1, before_x, h) for h in range(blocks_z)]
        for side in range(2):
            for step in range(DEGREE):
                start = step + 1 if side == 0 else DEGREE - step
                kz = [window(tiles[3][h][side], start) for h in range(blocks_z)]
                kzm = behind(kz, lane)
                for h in range(blocks_z):
                    pot = window(tiles[0][h][side], start)
                    kx = window(tiles[1][h][side], start)
                    ky = window(tiles[2][h][side], start)
                    kym = window(tiles[2][h][side], start - 1)
                    total = kx + window(kxm[h][side], start) + ky + kym + kz[h] + kzm[h]
                    inner, outer = (ky, kym) if side == 0 else (kym, ky)
                    coef_ref[side, step, 0, x, h] = unit * total + (2.0 * unit) * (pot - CENTRE)
                    coef_ref[side, step, 1, x, h] = unit * kx
                    coef_ref[side, step, 2, x, h] = unit * inner
                    coef_ref[side, step, 3, x, h] = unit * outer
                    coef_ref[side, step, 4, x, h] = unit * kz[h]
                    coef_ref[side, step, 5, x, h] = unit * kzm[h]


def edge_kernel(first_pair, k, odd_ref, ha_ref, hb_ref, coef_ref, seam_ref, sums_ref, edge_ref, gram_ref):
    members, rows_x, blocks_z = edge_ref.shape[:3]
    odd = odd_ref[0] == 1
    row, lane = iotas()
    upper = row < DEGREE

    def run(pair, side, w):
        turn, mark = (SUB - 1, row % DEGREE == DEGREE - 1) if side == 0 else (1, row % DEGREE == 0)
        last = None
        for step in range(DEGREE):
            seam = seam_ref.at[k * (members // 2) + pair, side, step]
            coef = coef_ref.at[side, step]
            centre, inner = [], []
            for x in range(rows_x):
                centre.append(
                    [jnp.where(mark, seam[0, x, h], pltpu.roll(w[x][h], turn, 0)) for h in range(blocks_z)]
                )
                inner.append(
                    [jnp.where(mark, seam[1, x, h], pltpu.roll(centre[x][h], turn, 0)) for h in range(blocks_z)]
                )
            fresh = []
            for x in range(rows_x):
                up_x, down_x = (x + 1) % rows_x, (x - 1) % rows_x
                front, back = ahead(centre[x], lane), behind(centre[x], lane)
                line = []
                for h in range(blocks_z):
                    total = coef[0, x, h] * centre[x][h]
                    total = total - coef[1, x, h] * centre[up_x][h]
                    total = total - coef[1, down_x, h] * centre[down_x][h]
                    total = total - coef[2, x, h] * inner[x][h]
                    total = total - coef[3, x, h] * w[x][h]
                    total = total - coef[4, x, h] * front[h]
                    total = total - coef[5, x, h] * back[h]
                    line.append(0.5 * total if step == 0 else total - last[x][h])
                fresh.append(line)
            last, w = inner, fresh
        return w

    def both(pair, carry):
        a = [[ha_ref[first_pair + pair, x, :, cut(h)] for h in range(blocks_z)] for x in range(rows_x)]
        b = [[hb_ref[first_pair + pair, x, :, cut(h)] for h in range(blocks_z)] for x in range(rows_x)]
        before = [[jnp.where(odd, a[x][h], b[x][h]) for h in range(blocks_z)] for x in range(rows_x)]
        top = run(pair, 0, before)
        after = [[jnp.where(odd, b[x][h], a[x][h]) for h in range(blocks_z)] for x in range(rows_x)]
        bottom = run(pair, 1, after)
        for x in range(rows_x):
            for h in range(blocks_z):
                edge_ref[2 * pair, x, h] = jnp.where(upper, top[x][h], pltpu.roll(bottom[x][h], DEGREE, 0))
                edge_ref[2 * pair + 1, x, h] = jnp.where(upper, pltpu.roll(top[x][h], DEGREE, 0), bottom[x][h])
        return carry

    lax.fori_loop(0, members // 2, both, 0)

    pairs = pairs_of(members)

    def gather(x, sums):
        sums = list(sums)
        for h in range(blocks_z):
            f = [edge_ref[a, x, h] for a in range(members)]
            for i, (a, b) in enumerate(pairs):
                sums[i] = sums[i] + f[a] * f[b]
        return tuple(sums)

    sums = lax.fori_loop(0, rows_x, gather, tuple(sums_ref[k, i] for i in range(len(pairs))))
    at = {pair: jnp.sum(s, axis=0, keepdims=True) for pair, s in zip(pairs, sums)}
    column_of = lax.broadcasted_iota(jnp.int32, (members, members), 1)
    gram = jnp.zeros((members, members), jnp.float32)
    for a in range(members):
        column = jnp.concatenate([at[min(a, b), max(a, b)] for b in range(members)], 0)
        gram = jnp.where(column_of == a, jnp.sum(column, axis=1, keepdims=True), gram)
    gram_ref[...] = gram


def assemble_kernel(body_ref, *refs):
    out_ref = refs[-1]
    count, rows_x, rows_y, depth = out_ref.shape
    row, _ = iotas()
    upper = row < DEGREE
    members = refs[0].shape[0]

    for k, edge_ref in enumerate(refs[:-1]):
        for a in range(members):
            for x in range(rows_x):
                for h in range(depth // LANES):
                    body, edge = body_ref[k * members + a, x, h], edge_ref[a, x, h]
                    out_ref[k * members + a, x, 0:SUB, cut(h)] = jnp.where(upper, edge, body)
                    out_ref[k * members + a, x, rows_y - SUB :, cut(h)] = jnp.where(upper, body, edge)


def density_kernel(body_ref, gram_ref, occ_ref, *refs):
    edge_refs, out_ref = refs[:-1], refs[-1]
    rows_x, rows_y, depth = out_ref.shape
    blocks, members, _ = gram_ref.shape
    row, _ = iotas()
    upper = row < DEGREE
    down = lax.broadcasted_iota(jnp.int32, (members, members), 0)
    along = lax.broadcasted_iota(jnp.int32, (members, members), 1)
    w = []
    for k in range(blocks):
        ratio = jnp.broadcast_to(occ_ref[k : k + 1, :], (members, members)) / (gram_ref[k] + EPSILON)
        column = jnp.sum(jnp.where(down == along, ratio, 0.0), axis=1, keepdims=True)
        w += [jnp.broadcast_to(column[a : a + 1, :], (SUB, LANES)) for a in range(members)]
    for x in range(rows_x):
        for h in range(depth // LANES):
            body = edge = None
            for k, edge_ref in enumerate(edge_refs):
                for a in range(members):
                    i = k * members + a
                    f, g = body_ref[i, x, h], edge_ref[a, x, h]
                    f, g = w[i] * (f * f), w[i] * (g * g)
                    body, edge = (f, g) if body is None else (body + f, edge + g)
            out_ref[x, 0:SUB, cut(h)] = jnp.where(upper, edge, body)
            out_ref[x, rows_y - SUB :, cut(h)] = jnp.where(upper, body, edge)


def vmem():
    return pl.BlockSpec(memory_space=pltpu.VMEM)


def smem():
    return pl.BlockSpec(memory_space=pltpu.SMEM)


def anywhere():
    return pl.BlockSpec(memory_space=pltpu.HBM)


def call(kernel, name, operands, outs, scratch=(), specs=None, place=jax.ShapeDtypeStruct, limit=8):
    shapes = tuple(place(shape, jnp.float32) for shape in outs)
    return pl.pallas_call(
        kernel,
        out_shape=shapes,
        in_specs=[vmem() for _ in operands] if specs is None else specs,
        out_specs=tuple(vmem() for _ in outs),
        scratch_shapes=[pltpu.VMEM(shape, jnp.float32) if isinstance(shape, tuple) else shape for shape in scratch],
        compiler_params=pltpu.CompilerParams(vmem_limit_bytes=limit * 1024 * 1024),
        name=name,
    )(*operands)


def fast_body(orbitals, potential, kinetic, occupations):
    blocks, members, _, rows_x, rows_y, depth = orbitals.shape
    count = blocks * members
    domains = lax.axis_size("grid")
    position = lax.axis_index("grid")
    parts = rows_y // SUB
    blocks_z = depth // LANES
    tile = (SUB, LANES)
    odd = (position % 2).astype(jnp.int32).reshape(1)

    pairs_a = [(i, i ^ 1) for i in range(domains)]
    pairs_b = [(i, (i + 1) % domains if i % 2 else (i - 1) % domains) for i in range(domains)]
    half = members // 2
    sizes = [half + (2 if k == 0 else 0) for k in range(blocks)]
    *packed, pot, kin, fields = call(
        functools.partial(pack_kernel, blocks),
        "pack",
        (
            odd,
            pltpu.with_memory_space_constraint(potential[0], pltpu.HBM),
            pltpu.with_memory_space_constraint(kinetic[:, 0], pltpu.HBM),
            pltpu.with_memory_space_constraint(orbitals.reshape(count, rows_x, rows_y, depth), pltpu.HBM),
        ),
        [(size, rows_x, SUB, depth) for size in sizes for _ in range(2)]
        + [(rows_x, rows_y, depth), (3, rows_x, rows_y, depth), (count, rows_x, rows_y, depth)],
        [pltpu.SemaphoreType.DMA((2 + blocks,))],
        specs=[smem()] + [anywhere()] * 3,
        place=pltpu.VMEM,
    )
    halos = [
        lax.ppermute(value, "grid", pairs_b if i % 2 else pairs_a) for i, value in enumerate(packed)
    ]

    body, seam, sums = call(
        functools.partial(interior_kernel, members),
        "interior",
        (pot, kin, fields),
        [
            (count, rows_x, blocks_z) + tile,
            (count // 2, 2, DEGREE, 2, rows_x, blocks_z) + tile,
            (blocks, len(pairs_of(members))) + tile,
        ],
        [
            (6, rows_x, parts, blocks_z) + tile,
            (4, rows_x, blocks_z, rows_y, LANES),
            (2, rows_x, blocks_z, rows_y, LANES),
        ],
    )
    (coef,) = call(
        windows_kernel,
        "windows",
        (odd, pot, kin, halos[0], halos[1]),
        [(2, DEGREE, 6, rows_x, blocks_z) + tile],
        specs=[smem()] + [vmem()] * 4,
    )
    edges, grams = [], []
    for k in range(blocks):
        edge, gram = call(
            functools.partial(edge_kernel, sizes[k] - half, k),
            "edge",
            (odd, halos[2 * k], halos[2 * k + 1], coef, seam, sums),
            [(members, rows_x, blocks_z) + tile, (members, members)],
            specs=[smem()] + [vmem()] * 5,
        )
        edges.append(edge)
        grams.append(gram)

    cells = rows_x * rows_y * depth * domains
    gram = jnp.stack(grams) * (1.0 / cells)
    bit = 1
    while bit < domains:
        gram = gram + swapped(gram, "grid", bit)
        bit *= 2

    (filtered,) = call(assemble_kernel, "assemble", (body, *edges), [fields.shape])
    (partial_value,) = call(density_kernel, "density", (body, gram, occupations, *edges), [pot.shape])

    bands = lax.axis_size("band")
    band = lax.axis_index("band")
    share = rows_y // bands
    value = partial_value.reshape(rows_x, bands, share, depth)
    bit = 1
    width = bands
    while bit < bands:
        value = value.reshape(rows_x, width // 2, 2, share, depth)
        mine = (band // bit) % 2
        keep = lax.dynamic_index_in_dim(value, mine, 2, False)
        send = lax.dynamic_index_in_dim(value, 1 - mine, 2, False)
        value = keep + swapped(send, "band", bit)
        bit *= 2
        width //= 2
    density = value.reshape(1, rows_x, share, depth)
    return filtered.reshape(orbitals.shape), gram, density


def extend(field, width, across):
    lower = shifted(field[..., -width:, :, :], "grid", across)
    upper = shifted(field[..., :width, :, :], "grid", -across)
    widened = jnp.concatenate([lower, field, upper], -3)
    column = lax.axis_index("grid") % across
    left_plain = shifted(widened[..., :, -width:, :], "grid", 1)
    left_wrap = shifted(widened[..., :, -width:, :], "grid", -(across - 1))
    left = jnp.where(column == 0, left_wrap, left_plain)
    right_plain = shifted(widened[..., :, :width, :], "grid", -1)
    right_wrap = shifted(widened[..., :, :width, :], "grid", across - 1)
    right = jnp.where(column == across - 1, right_wrap, right_plain)
    return jnp.concatenate([left, widened, right], -2)


def hamilton(field, coeffs):
    inner = field[..., 1:-1, 1:-1, :]
    kin_x = coeffs[1]
    total = kin_x[1:-1, 1:-1] * (inner - field[..., 2:, 1:-1, :])
    total = total + kin_x[:-2, 1:-1] * (inner - field[..., :-2, 1:-1, :])
    kin_y = coeffs[2]
    total = total + kin_y[1:-1, 1:-1] * (inner - field[..., 1:-1, 2:, :])
    total = total + kin_y[1:-1, :-2] * (inner - field[..., 1:-1, :-2, :])
    kin_z = coeffs[3, 1:-1, 1:-1]
    total = total + kin_z * (inner - jnp.roll(inner, -1, -1))
    total = total + jnp.roll(kin_z, 1, -1) * (inner - jnp.roll(inner, 1, -1))
    return 0.5 * total + coeffs[0, 1:-1, 1:-1] * inner


def general_body(across, orbitals, potential, kinetic, occupations):
    blocks = orbitals.shape[0]
    members = orbitals.shape[1]
    rows_x = orbitals.shape[3]
    rows_y = orbitals.shape[4]
    coeffs = jnp.concatenate([potential, kinetic[:, 0]], 0)
    current = orbitals[:, :, 0]
    previous = current
    coeff_ext = None
    for degree_step in range(DEGREE):
        if degree_step == 0:
            stacked = jnp.concatenate(
                [coeffs, current.reshape((blocks * members,) + current.shape[2:])], 0
            )
            wide = extend(stacked, 1, across)
            coeff_ext = wide[:4]
            extended = wide[4:].reshape((blocks, members) + wide.shape[1:])
        else:
            extended = extend(current, 1, across)
        image = hamilton(extended, coeff_ext)
        inner = extended[..., 1:-1, 1:-1, :]
        if degree_step == 0:
            fresh = (image - CENTRE * inner) / HALF_WIDTH
        else:
            fresh = 2.0 / HALF_WIDTH * (image - CENTRE * inner) - previous
        previous = current
        current = fresh
    cells = rows_x * rows_y * orbitals.shape[5] * lax.axis_size("grid")
    flat = current.reshape(blocks, members, -1)
    local_gram = jnp.einsum("kbx,kcx->kbc", flat, flat, precision=lax.Precision.HIGHEST) / cells
    gram = lax.psum(local_gram, "grid")
    diagonal = jnp.diagonal(gram, axis1=1, axis2=2)
    weight = occupations / (diagonal + EPSILON)
    partial_value = jnp.einsum(
        "kb,kbxyz->xyz", weight, current * current, precision=lax.Precision.HIGHEST
    )
    density = lax.psum_scatter(partial_value[None], "band", scatter_dimension=2, tiled=True)
    return (current[:, :, None], gram, density)


def solution(mesh):
    domains = mesh.shape["grid"]
    across = min(domains, 8)
    if domains == across and domains & (domains - 1) == 0 and domains > 1:
        body = fast_body
    else:
        body = functools.partial(general_body, across)
    placed = (
        P("band", None, "grid", None, None, None),
        P("grid", None, None, None),
        P(None, "grid", None, None, None),
        P("band", None),
    )
    return jax.shard_map(
        body,
        mesh=mesh,
        in_specs=placed,
        out_specs=(
            P("band", None, "grid", None, None, None),
            P("band", None, None),
            P("grid", None, "band", None),
        ),
        check_vma=False,
    )
```

```python
import functools

import jax
import jax.numpy as jnp
from jax import lax
from jax.experimental import pallas as pl
from jax.experimental.pallas import tpu as pltpu
from jax.sharding import PartitionSpec as P

DEGREE = 4

CENTRE = 6.0
HALF_WIDTH = 4.0
EPSILON = 1e-06
SUB = 8
LANES = 128


def shifted(value, axis, steps):
    count = lax.axis_size(axis)
    pairs = [(source, (source + steps) % count) for source in range(count)]
    return lax.ppermute(value, axis, pairs)


def swapped(value, axis, bit):
    count = lax.axis_size(axis)
    return lax.ppermute(value, axis, [(i, i ^ bit) for i in range(count)])


def cut(h):
    return slice(LANES * h, LANES * (h + 1))


def iotas():
    return tuple(lax.broadcasted_iota(jnp.int32, (SUB, LANES), axis) for axis in range(2))


def ahead(line, lane):
    turned = [pltpu.roll(block, LANES - 1, 1) for block in line]
    return [jnp.where(lane == LANES - 1, turned[(h + 1) % len(line)], turned[h]) for h in range(len(line))]


def behind(line, lane):
    turned = [pltpu.roll(block, 1, 1) for block in line]
    return [jnp.where(lane == 0, turned[h - 1], turned[h]) for h in range(len(line))]


def pack_kernel(steps, odd_ref, pot_any, kin_any, orb_any, *refs):
    arrivals = refs[-1]
    pot_ref, kin_ref, orb_ref = refs[-4:-1]
    out_refs = refs[:-4]
    count, rows_x, rows_y, depth = orb_ref.shape
    odd = odd_ref[0] == 1
    row, _ = iotas()
    upper = row < DEGREE
    loads = [
        pltpu.make_async_copy(pot_any, pot_ref, arrivals.at[0]),
        pltpu.make_async_copy(kin_any, kin_ref, arrivals.at[1]),
    ]
    size = count // steps
    for k in range(steps):
        part = pl.ds(k * size, size)
        loads.append(pltpu.make_async_copy(orb_any.at[part], orb_ref.at[part], arrivals.at[2 + k]))
    for load in loads:
        load.start()
    fields = [pot_ref] + [kin_ref.at[c] for c in range(3)] + [orb_ref.at[m] for m in range(count)]
    place = 0
    for index in range(0, len(out_refs), 2):
        a_ref, b_ref = out_refs[index : index + 2]
        if index == 0:
            loads[0].wait()
            loads[1].wait()
        loads[2 + index // 2].wait()
        for p in range(a_ref.shape[0]):
            one, two = fields[place], fields[place + 1]
            place += 2
            for x in range(rows_x):
                for h in range(depth // LANES):
                    first = jnp.where(upper, one[x, 0:SUB, cut(h)], pltpu.roll(two[x, 0:SUB, cut(h)], DEGREE, 0))
                    tail = slice(rows_y - SUB, rows_y)
                    last = jnp.where(upper, pltpu.roll(one[x, tail, cut(h)], DEGREE, 0), two[x, tail, cut(h)])
                    a_ref[p, x, :, cut(h)] = jnp.where(odd, first, last)
                    b_ref[p, x, :, cut(h)] = jnp.where(odd, last, first)


def ring_tiles(ref, index, parts):
    return [
        [ref[index + (h, pl.ds(t, SUB, stride=parts), slice(None))] for h in range(ref.shape[-3])]
        for t in range(parts)
    ]


def own_coefficients(pot_ref, kin_ref, coef_ref, ring, lane):
    rows_x, rows_y, depth = pot_ref.shape
    parts = rows_y // SUB
    unit = 1.0 / HALF_WIDTH
    for x in range(rows_x):
        for c in range(4):
            own_ref = pot_ref if c == 0 else kin_ref.at[c - 1]
            for h in range(depth // LANES):
                ring[c, x, h] = own_ref[x, :, cut(h)]
    for x in range(rows_x):
        before = (x - 1) % rows_x
        pot = ring_tiles(ring, (0, x), parts)
        kx = ring_tiles(ring, (1, x), parts)
        kxm = ring_tiles(ring, (1, before), parts)
        ky = ring_tiles(ring, (2, x), parts)
        kz = ring_tiles(ring, (3, x), parts)
        for t in range(parts):
            kzm = behind(kz[t], lane)
            for h in range(depth // LANES):
                kym = ky[t - 1][h] if t > 0 else pltpu.roll(ky[parts - 1][h], 1, 0)
                total = kx[t][h] + kxm[t][h] + ky[t][h] + kym + kz[t][h] + kzm[h]
                coef_ref[0, x, t, h] = unit * total + (2.0 * unit) * (pot[t][h] - CENTRE)
                coef_ref[1, x, t, h] = unit * kx[t][h]
                coef_ref[2, x, t, h] = unit * ky[t][h]
                coef_ref[3, x, t, h] = unit * kz[t][h]
                coef_ref[4, x, t, h] = unit * kzm[h]
                if t == 0:
                    coef_ref[5, x, 0, h] = unit * kym


def apply_own(coef_ref, v, x, t, lane):
    rows_x, parts = len(v), len(v[0])
    up_x, down_x = (x + 1) % rows_x, (x - 1) % rows_x
    own = v[x][t]
    front, back = ahead(own, lane), behind(own, lane)
    result = []
    for h in range(len(own)):
        total = coef_ref[0, x, t, h] * own[h]
        total = total - coef_ref[1, x, t, h] * v[up_x][t][h]
        total = total - coef_ref[1, down_x, t, h] * v[down_x][t][h]
        above = v[x][t + 1][h] if t < parts - 1 else pltpu.roll(v[x][0][h], SUB - 1, 0)
        total = total - coef_ref[2, x, t, h] * above
        if t > 0:
            total = total - coef_ref[2, x, t - 1, h] * v[x][t - 1][h]
        else:
            total = total - coef_ref[5, x, 0, h] * pltpu.roll(v[x][parts - 1][h], 1, 0)
        total = total - coef_ref[3, x, t, h] * front[h]
        result.append(total - coef_ref[4, x, t, h] * back[h])
    return result


def pairs_of(members):
    return [(a, b) for a in range(members) for b in range(a, members)]


def interior_kernel(members, pot_ref, kin_ref, orb_ref, body_ref, seam_ref, sums_ref, coef_ref, coef_ring, ring):
    count, rows_x, rows_y, depth = orb_ref.shape
    parts = rows_y // SUB
    blocks_z = depth // LANES
    row, lane = iotas()
    upper = row < DEGREE
    own_coefficients(pot_ref, kin_ref, coef_ref, coef_ring, lane)

    def one(pair, half):
        m = 2 * pair + half
        for x in range(rows_x):
            for h in range(blocks_z):
                ring[half, x, h] = orb_ref[m, x, :, cut(h)]
        v = [ring_tiles(ring.at[half], (x,), parts) for x in range(rows_x)]
        previous = None
        for step in range(DEGREE):
            for x in range(rows_x):
                for h in range(blocks_z):
                    for side in range(2):
                        for depth_in in range(2):
                            y = step + depth_in if side == 0 else rows_y - 1 - step - depth_in
                            place = DEGREE * half + (DEGREE - 1 if side == 0 else 0)
                            value = v[x][y % parts][h][y // parts : y // parts + 1]
                            seam_ref[pair, side, step, depth_in, x, h, place : place + 1, :] = value
            fresh = []
            for x in range(rows_x):
                rows = []
                for t in range(parts):
                    image = apply_own(coef_ref, v, x, t, lane)
                    if step == 0:
                        rows.append([0.5 * i for i in image])
                    else:
                        rows.append([i - p for i, p in zip(image, previous[x][t])])
                fresh.append(rows)
            previous, v = v, fresh
        for x in range(rows_x):
            for t in range(parts):
                for h in range(blocks_z):
                    ring[half, x, h, pl.ds(t, SUB, stride=parts), :] = v[x][t][h]
        for x in range(rows_x):
            for h in range(blocks_z):
                body_ref[m, x, h] = jnp.where(upper, ring[half, x, h, rows_y - SUB :], ring[half, x, h, 0:SUB])

    def both(pair, carry):
        one(pair, 0)
        one(pair, 1)
        return carry

    lax.fori_loop(0, count // 2, both, 0, unroll=True)

    pairs = pairs_of(members)
    for k in range(count // members):

        def gather(x, sums, k=k):
            sums = list(sums)
            for h in range(blocks_z):
                f = [body_ref[k * members + a, x, h] for a in range(members)]
                for i, (a, b) in enumerate(pairs):
                    sums[i] = sums[i] + f[a] * f[b]
            return tuple(sums)

        sums = lax.fori_loop(0, rows_x, gather, tuple(jnp.zeros((SUB, LANES), jnp.float32) for _ in pairs), unroll=True)
        for i, value in enumerate(sums):
            sums_ref[k, i] = value


def windows_kernel(odd_ref, pot_ref, kin_ref, ha_ref, hb_ref, coef_ref):
    rows_x, rows_y, depth = pot_ref.shape
    odd = odd_ref[0] == 1
    row, lane = iotas()
    upper = row < DEGREE
    blocks_z = depth // LANES
    unit = 1.0 / HALF_WIDTH

    def window(tile, start):
        low = pltpu.roll(tile, (SUB - start) % SUB, 0) if start % SUB else tile
        high = pltpu.roll(tile, (SUB + DEGREE - start) % SUB, 0) if (DEGREE - start) % SUB else tile
        return jnp.where(upper, low, high)

    def field(c, x, h):
        own_ref = pot_ref if c == 0 else kin_ref.at[c - 1]
        a, b = ha_ref[c // 2, x, :, cut(h)], hb_ref[c // 2, x, :, cut(h)]
        before, after = jnp.where(odd, a, b), jnp.where(odd, b, a)
        head, tail = own_ref[x, 0:SUB, cut(h)], own_ref[x, rows_y - SUB :, cut(h)]
        if c % 2:
            before = pltpu.roll(before, DEGREE, 0)
        top = jnp.where(upper, before, pltpu.roll(head, DEGREE, 0))
        if c % 2:
            after = pltpu.roll(after, DEGREE, 0)
        kept = pltpu.roll(tail, SUB - (DEGREE - 1), 0)
        bottom = jnp.where(row < DEGREE + 1, kept, pltpu.roll(after, DEGREE + 1, 0))
        return top, bottom

    for x in range(rows_x):
        before_x = (x - 1) % rows_x
        tiles = [[field(c, x, h) for h in range(blocks_z)] for c in range(4)]
        kxm = [field(1, before_x, h) for h in range(blocks_z)]
        for side in range(2):
            for step in range(DEGREE):
                start = step + 1 if side == 0 else DEGREE - step
                kz = [window(tiles[3][h][side], start) for h in range(blocks_z)]
                kzm = behind(kz, lane)
                for h in range(blocks_z):
                    pot = window(tiles[0][h][side], start)
                    kx = window(tiles[1][h][side], start)
                    ky = window(tiles[2][h][side], start)
                    kym = window(tiles[2][h][side], start - 1)
                    total = kx + window(kxm[h][side], start) + ky + kym + kz[h] + kzm[h]
                    inner, outer = (ky, kym) if side == 0 else (kym, ky)
                    coef_ref[side, step, 0, x, h] = unit * total + (2.0 * unit) * (pot - CENTRE)
                    coef_ref[side, step, 1, x, h] = unit * kx
                    coef_ref[side, step, 2, x, h] = unit * inner
                    coef_ref[side, step, 3, x, h] = unit * outer
                    coef_ref[side, step, 4, x, h] = unit * kz[h]
                    coef_ref[side, step, 5, x, h] = unit * kzm[h]


def edge_kernel(first_pair, k, odd_ref, ha_ref, hb_ref, coef_ref, seam_ref, sums_ref, edge_ref, gram_ref):
    members, rows_x, blocks_z = edge_ref.shape[:3]
    odd = odd_ref[0] == 1
    row, lane = iotas()
    upper = row < DEGREE

    def run(pair, side, w):
        turn, mark = (SUB - 1, row % DEGREE == DEGREE - 1) if side == 0 else (1, row % DEGREE == 0)
        last = None
        for step in range(DEGREE):
            seam = seam_ref.at[k * (members // 2) + pair, side, step]
            coef = coef_ref.at[side, step]
            centre, inner = [], []
            for x in range(rows_x):
                centre.append(
                    [jnp.where(mark, seam[0, x, h], pltpu.roll(w[x][h], turn, 0)) for h in range(blocks_z)]
                )
                inner.append(
                    [jnp.where(mark, seam[1, x, h], pltpu.roll(centre[x][h], turn, 0)) for h in range(blocks_z)]
                )
            fresh = []
            for x in range(rows_x):
                up_x, down_x = (x + 1) % rows_x, (x - 1) % rows_x
                front, back = ahead(centre[x], lane), behind(centre[x], lane)
                line = []
                for h in range(blocks_z):
                    total = coef[0, x, h] * centre[x][h]
                    total = total - coef[1, x, h] * centre[up_x][h]
                    total = total - coef[1, down_x, h] * centre[down_x][h]
                    total = total - coef[2, x, h] * inner[x][h]
                    total = total - coef[3, x, h] * w[x][h]
                    total = total - coef[4, x, h] * front[h]
                    total = total - coef[5, x, h] * back[h]
                    line.append(0.5 * total if step == 0 else total - last[x][h])
                fresh.append(line)
            last, w = inner, fresh
        return w

    def both(pair, carry):
        a = [[ha_ref[first_pair + pair, x, :, cut(h)] for h in range(blocks_z)] for x in range(rows_x)]
        b = [[hb_ref[first_pair + pair, x, :, cut(h)] for h in range(blocks_z)] for x in range(rows_x)]
        before = [[jnp.where(odd, a[x][h], b[x][h]) for h in range(blocks_z)] for x in range(rows_x)]
        top = run(pair, 0, before)
        after = [[jnp.where(odd, b[x][h], a[x][h]) for h in range(blocks_z)] for x in range(rows_x)]
        bottom = run(pair, 1, after)
        for x in range(rows_x):
            for h in range(blocks_z):
                edge_ref[2 * pair, x, h] = jnp.where(upper, top[x][h], pltpu.roll(bottom[x][h], DEGREE, 0))
                edge_ref[2 * pair + 1, x, h] = jnp.where(upper, pltpu.roll(top[x][h], DEGREE, 0), bottom[x][h])
        return carry

    lax.fori_loop(0, members // 2, both, 0, unroll=True)

    pairs = pairs_of(members)

    def gather(x, sums):
        sums = list(sums)
        for h in range(blocks_z):
            f = [edge_ref[a, x, h] for a in range(members)]
            for i, (a, b) in enumerate(pairs):
                sums[i] = sums[i] + f[a] * f[b]
        return tuple(sums)

    sums = lax.fori_loop(0, rows_x, gather, tuple(sums_ref[k, i] for i in range(len(pairs))), unroll=True)
    at = {pair: jnp.sum(s, axis=0, keepdims=True) for pair, s in zip(pairs, sums)}
    column_of = lax.broadcasted_iota(jnp.int32, (members, members), 1)
    gram = jnp.zeros((members, members), jnp.float32)
    for a in range(members):
        column = jnp.concatenate([at[min(a, b), max(a, b)] for b in range(members)], 0)
        gram = jnp.where(column_of == a, jnp.sum(column, axis=1, keepdims=True), gram)
    gram_ref[...] = gram


def assemble_kernel(body_ref, *refs):
    out_ref = refs[-1]
    count, rows_x, rows_y, depth = out_ref.shape
    row, _ = iotas()
    upper = row < DEGREE
    members = refs[0].shape[0]

    for k, edge_ref in enumerate(refs[:-1]):
        for a in range(members):
            for x in range(rows_x):
                for h in range(depth // LANES):
                    body, edge = body_ref[k * members + a, x, h], edge_ref[a, x, h]
                    out_ref[k * members + a, x, 0:SUB, cut(h)] = jnp.where(upper, edge, body)
                    out_ref[k * members + a, x, rows_y - SUB :, cut(h)] = jnp.where(upper, body, edge)


def density_kernel(body_ref, gram_ref, occ_ref, *refs):
    edge_refs, out_ref = refs[:-1], refs[-1]
    rows_x, rows_y, depth = out_ref.shape
    blocks, members, _ = gram_ref.shape
    row, _ = iotas()
    upper = row < DEGREE
    down = lax.broadcasted_iota(jnp.int32, (members, members), 0)
    along = lax.broadcasted_iota(jnp.int32, (members, members), 1)
    w = []
    for k in range(blocks):
        ratio = jnp.broadcast_to(occ_ref[k : k + 1, :], (members, members)) / (gram_ref[k] + EPSILON)
        column = jnp.sum(jnp.where(down == along, ratio, 0.0), axis=1, keepdims=True)
        w += [jnp.broadcast_to(column[a : a + 1, :], (SUB, LANES)) for a in range(members)]
    for x in range(rows_x):
        for h in range(depth // LANES):
            body = edge = None
            for k, edge_ref in enumerate(edge_refs):
                for a in range(members):
                    i = k * members + a
                    f, g = body_ref[i, x, h], edge_ref[a, x, h]
                    f, g = w[i] * (f * f), w[i] * (g * g)
                    body, edge = (f, g) if body is None else (body + f, edge + g)
            out_ref[x, 0:SUB, cut(h)] = jnp.where(upper, edge, body)
            out_ref[x, rows_y - SUB :, cut(h)] = jnp.where(upper, body, edge)


def vmem():
    return pl.BlockSpec(memory_space=pltpu.VMEM)


def smem():
    return pl.BlockSpec(memory_space=pltpu.SMEM)


def anywhere():
    return pl.BlockSpec(memory_space=pltpu.HBM)


def call(kernel, name, operands, outs, scratch=(), specs=None, place=jax.ShapeDtypeStruct, limit=8):
    shapes = tuple(place(shape, jnp.float32) for shape in outs)
    return pl.pallas_call(
        kernel,
        out_shape=shapes,
        in_specs=[vmem() for _ in operands] if specs is None else specs,
        out_specs=tuple(vmem() for _ in outs),
        scratch_shapes=[pltpu.VMEM(shape, jnp.float32) if isinstance(shape, tuple) else shape for shape in scratch],
        compiler_params=pltpu.CompilerParams(vmem_limit_bytes=limit * 1024 * 1024),
        name=name,
    )(*operands)


def fast_body(orbitals, potential, kinetic, occupations):
    blocks, members, _, rows_x, rows_y, depth = orbitals.shape
    count = blocks * members
    domains = lax.axis_size("grid")
    position = lax.axis_index("grid")
    parts = rows_y // SUB
    blocks_z = depth // LANES
    tile = (SUB, LANES)
    odd = (position % 2).astype(jnp.int32).reshape(1)

    pairs_a = [(i, i ^ 1) for i in range(domains)]
    pairs_b = [(i, (i + 1) % domains if i % 2 else (i - 1) % domains) for i in range(domains)]
    half = members // 2
    sizes = [half + (2 if k == 0 else 0) for k in range(blocks)]
    *packed, pot, kin, fields = call(
        functools.partial(pack_kernel, blocks),
        "pack",
        (
            odd,
            pltpu.with_memory_space_constraint(potential[0], pltpu.HBM),
            pltpu.with_memory_space_constraint(kinetic[:, 0], pltpu.HBM),
            pltpu.with_memory_space_constraint(orbitals.reshape(count, rows_x, rows_y, depth), pltpu.HBM),
        ),
        [(size, rows_x, SUB, depth) for size in sizes for _ in range(2)]
        + [(rows_x, rows_y, depth), (3, rows_x, rows_y, depth), (count, rows_x, rows_y, depth)],
        [pltpu.SemaphoreType.DMA((2 + blocks,))],
        specs=[smem()] + [anywhere()] * 3,
        place=pltpu.VMEM,
    )
    halos = [
        lax.ppermute(value, "grid", pairs_b if i % 2 else pairs_a) for i, value in enumerate(packed)
    ]

    body, seam, sums = call(
        functools.partial(interior_kernel, members),
        "interior",
        (pot, kin, fields),
        [
            (count, rows_x, blocks_z) + tile,
            (count // 2, 2, DEGREE, 2, rows_x, blocks_z) + tile,
            (blocks, len(pairs_of(members))) + tile,
        ],
        [
            (6, rows_x, parts, blocks_z) + tile,
            (4, rows_x, blocks_z, rows_y, LANES),
            (2, rows_x, blocks_z, rows_y, LANES),
        ],
    )
    (coef,) = call(
        windows_kernel,
        "windows",
        (odd, pot, kin, halos[0], halos[1]),
        [(2, DEGREE, 6, rows_x, blocks_z) + tile],
        specs=[smem()] + [vmem()] * 4,
    )
    edges, grams = [], []
    for k in range(blocks):
        edge, gram = call(
            functools.partial(edge_kernel, sizes[k] - half, k),
            "edge",
            (odd, halos[2 * k], halos[2 * k + 1], coef, seam, sums),
            [(members, rows_x, blocks_z) + tile, (members, members)],
            specs=[smem()] + [vmem()] * 5,
        )
        edges.append(edge)
        grams.append(gram)

    cells = rows_x * rows_y * depth * domains
    gram = jnp.stack(grams) * (1.0 / cells)
    bit = 1
    while bit < domains:
        gram = gram + swapped(gram, "grid", bit)
        bit *= 2

    (filtered,) = call(assemble_kernel, "assemble", (body, *edges), [fields.shape])
    (partial_value,) = call(density_kernel, "density", (body, gram, occupations, *edges), [pot.shape])

    bands = lax.axis_size("band")
    band = lax.axis_index("band")
    share = rows_y // bands
    value = partial_value.reshape(rows_x, bands, share, depth)
    bit = 1
    width = bands
    while bit < bands:
        value = value.reshape(rows_x, width // 2, 2, share, depth)
        mine = (band // bit) % 2
        keep = lax.dynamic_index_in_dim(value, mine, 2, False)
        send = lax.dynamic_index_in_dim(value, 1 - mine, 2, False)
        value = keep + swapped(send, "band", bit)
        bit *= 2
        width //= 2
    density = value.reshape(1, rows_x, share, depth)
    return filtered.reshape(orbitals.shape), gram, density


def extend(field, width, across):
    lower = shifted(field[..., -width:, :, :], "grid", across)
    upper = shifted(field[..., :width, :, :], "grid", -across)
    widened = jnp.concatenate([lower, field, upper], -3)
    column = lax.axis_index("grid") % across
    left_plain = shifted(widened[..., :, -width:, :], "grid", 1)
    left_wrap = shifted(widened[..., :, -width:, :], "grid", -(across - 1))
    left = jnp.where(column == 0, left_wrap, left_plain)
    right_plain = shifted(widened[..., :, :width, :], "grid", -1)
    right_wrap = shifted(widened[..., :, :width, :], "grid", across - 1)
    right = jnp.where(column == across - 1, right_wrap, right_plain)
    return jnp.concatenate([left, widened, right], -2)


def hamilton(field, coeffs):
    inner = field[..., 1:-1, 1:-1, :]
    kin_x = coeffs[1]
    total = kin_x[1:-1, 1:-1] * (inner - field[..., 2:, 1:-1, :])
    total = total + kin_x[:-2, 1:-1] * (inner - field[..., :-2, 1:-1, :])
    kin_y = coeffs[2]
    total = total + kin_y[1:-1, 1:-1] * (inner - field[..., 1:-1, 2:, :])
    total = total + kin_y[1:-1, :-2] * (inner - field[..., 1:-1, :-2, :])
    kin_z = coeffs[3, 1:-1, 1:-1]
    total = total + kin_z * (inner - jnp.roll(inner, -1, -1))
    total = total + jnp.roll(kin_z, 1, -1) * (inner - jnp.roll(inner, 1, -1))
    return 0.5 * total + coeffs[0, 1:-1, 1:-1] * inner


def general_body(across, orbitals, potential, kinetic, occupations):
    blocks = orbitals.shape[0]
    members = orbitals.shape[1]
    rows_x = orbitals.shape[3]
    rows_y = orbitals.shape[4]
    coeffs = jnp.concatenate([potential, kinetic[:, 0]], 0)
    current = orbitals[:, :, 0]
    previous = current
    coeff_ext = None
    for degree_step in range(DEGREE):
        if degree_step == 0:
            stacked = jnp.concatenate(
                [coeffs, current.reshape((blocks * members,) + current.shape[2:])], 0
            )
            wide = extend(stacked, 1, across)
            coeff_ext = wide[:4]
            extended = wide[4:].reshape((blocks, members) + wide.shape[1:])
        else:
            extended = extend(current, 1, across)
        image = hamilton(extended, coeff_ext)
        inner = extended[..., 1:-1, 1:-1, :]
        if degree_step == 0:
            fresh = (image - CENTRE * inner) / HALF_WIDTH
        else:
            fresh = 2.0 / HALF_WIDTH * (image - CENTRE * inner) - previous
        previous = current
        current = fresh
    cells = rows_x * rows_y * orbitals.shape[5] * lax.axis_size("grid")
    flat = current.reshape(blocks, members, -1)
    local_gram = jnp.einsum("kbx,kcx->kbc", flat, flat, precision=lax.Precision.HIGHEST) / cells
    gram = lax.psum(local_gram, "grid")
    diagonal = jnp.diagonal(gram, axis1=1, axis2=2)
    weight = occupations / (diagonal + EPSILON)
    partial_value = jnp.einsum(
        "kb,kbxyz->xyz", weight, current * current, precision=lax.Precision.HIGHEST
    )
    density = lax.psum_scatter(partial_value[None], "band", scatter_dimension=2, tiled=True)
    return (current[:, :, None], gram, density)


def solution(mesh):
    domains = mesh.shape["grid"]
    across = min(domains, 8)
    if domains == across and domains & (domains - 1) == 0 and domains > 1:
        body = fast_body
    else:
        body = functools.partial(general_body, across)
    placed = (
        P("band", None, "grid", None, None, None),
        P("grid", None, None, None),
        P(None, "grid", None, None, None),
        P("band", None),
    )
    return jax.shard_map(
        body,
        mesh=mesh,
        in_specs=placed,
        out_specs=(
            P("band", None, "grid", None, None, None),
            P("band", None, None),
            P("grid", None, "band", None),
        ),
        check_vma=False,
    )
```

```python
import functools

import jax
import jax.numpy as jnp
from jax import lax
from jax.experimental import pallas as pl
from jax.experimental.pallas import tpu as pltpu
from jax.sharding import PartitionSpec as P


DEGREE = 4

CENTRE = 6.0
HALF_WIDTH = 4.0
EPSILON = 1e-06
SUB = 8
LANES = 128


def shifted(value, axis, steps):
    count = lax.axis_size(axis)
    pairs = [(source, (source + steps) % count) for source in range(count)]
    return lax.ppermute(value, axis, pairs)


def swapped(value, axis, bit):
    count = lax.axis_size(axis)
    return lax.ppermute(value, axis, [(i, i ^ bit) for i in range(count)])


def cut(h):
    return slice(LANES * h, LANES * (h + 1))


def iotas():
    return tuple(lax.broadcasted_iota(jnp.int32, (SUB, LANES), axis) for axis in range(2))


def ahead(line, lane):
    turned = [pltpu.roll(block, LANES - 1, 1) for block in line]
    return [jnp.where(lane == LANES - 1, turned[(h + 1) % len(line)], turned[h]) for h in range(len(line))]


def behind(line, lane):
    turned = [pltpu.roll(block, 1, 1) for block in line]
    return [jnp.where(lane == 0, turned[h - 1], turned[h]) for h in range(len(line))]


def pack_kernel(blocks, odd_ref, pot_any, kin_any, orb_any, *refs):
    a_refs, b_ref = refs[:blocks], refs[blocks]
    pot_ref, kin_ref, orb_ref, arrivals = refs[blocks + 1 :]
    count, rows_x, rows_y, depth = orb_ref.shape
    odd = odd_ref[0] == 1
    row, _ = iotas()
    upper = row < DEGREE
    size = count // blocks
    loads = [pltpu.make_async_copy(pot_any, pot_ref, arrivals.at[0]), pltpu.make_async_copy(kin_any, kin_ref, arrivals.at[1])]
    for k in range(blocks):
        part = pl.ds(k * size, size)
        loads.append(pltpu.make_async_copy(orb_any.at[part], orb_ref.at[part], arrivals.at[2 + k]))
    for load in loads:
        load.start()

    def edges(one, two, x, h):
        tail = slice(rows_y - SUB, rows_y)
        first = jnp.where(upper, one[x, 0:SUB, cut(h)], pltpu.roll(two[x, 0:SUB, cut(h)], DEGREE, 0))
        last = jnp.where(upper, pltpu.roll(one[x, tail, cut(h)], DEGREE, 0), two[x, tail, cut(h)])
        return jnp.where(odd, first, last), jnp.where(odd, last, first)

    places = [(x, h) for x in range(rows_x) for h in range(depth // LANES)]
    loads[0].wait()
    loads[1].wait()
    for x, h in places:
        low_a, low_b = edges(pot_ref, kin_ref.at[0], x, h)
        high_a, high_b = edges(kin_ref.at[1], kin_ref.at[2], x, h)
        a_refs[0][0, x, :, cut(h)] = low_a
        a_refs[0][1, x, :, cut(h)] = high_a
        b_ref[0, x, :, cut(h)] = low_b
        b_ref[1, x, :, cut(h)] = high_b
    for k in range(blocks):
        loads[2 + k].wait()
        for p in range(size // 2):
            m = k * size + 2 * p
            for x, h in places:
                a, b = edges(orb_ref.at[m], orb_ref.at[m + 1], x, h)
                a_refs[k][(0 if k else 2) + p, x, :, cut(h)] = a
                b_ref[2 + m // 2, x, :, cut(h)] = b


def ring_tiles(ref, index, parts):
    return [
        [ref[index + (h, pl.ds(t, SUB, stride=parts), slice(None))] for h in range(ref.shape[-3])]
        for t in range(parts)
    ]


def own_coefficients(pot_ref, kin_ref, coef_ref, ring, lane):
    rows_x, rows_y, depth = pot_ref.shape
    parts = rows_y // SUB
    unit = 1.0 / HALF_WIDTH
    for x in range(rows_x):
        for c in range(4):
            own_ref = pot_ref if c == 0 else kin_ref.at[c - 1]
            for h in range(depth // LANES):
                ring[c, x, h] = own_ref[x, :, cut(h)]
    for x in range(rows_x):
        before = (x - 1) % rows_x
        pot = ring_tiles(ring, (0, x), parts)
        kx = ring_tiles(ring, (1, x), parts)
        kxm = ring_tiles(ring, (1, before), parts)
        ky = ring_tiles(ring, (2, x), parts)
        kz = ring_tiles(ring, (3, x), parts)
        for t in range(parts):
            kzm = behind(kz[t], lane)
            for h in range(depth // LANES):
                kym = ky[t - 1][h] if t > 0 else pltpu.roll(ky[parts - 1][h], 1, 0)
                total = kx[t][h] + kxm[t][h] + ky[t][h] + kym + kz[t][h] + kzm[h]
                coef_ref[0, x, t, h] = unit * total + (2.0 * unit) * (pot[t][h] - CENTRE)
                coef_ref[1, x, t, h] = unit * kx[t][h]
                coef_ref[2, x, t, h] = unit * ky[t][h]
                coef_ref[3, x, t, h] = unit * kz[t][h]
                coef_ref[4, x, t, h] = unit * kzm[h]
                if t == 0:
                    coef_ref[5, x, 0, h] = unit * kym


def apply_own(coef_ref, v, x, t, lane):
    rows_x, parts = len(v), len(v[0])
    up_x, down_x = (x + 1) % rows_x, (x - 1) % rows_x
    own = v[x][t]
    front, back = ahead(own, lane), behind(own, lane)
    result = []
    for h in range(len(own)):
        total = coef_ref[0, x, t, h] * own[h]
        total = total - coef_ref[1, x, t, h] * v[up_x][t][h]
        total = total - coef_ref[1, down_x, t, h] * v[down_x][t][h]
        above = v[x][t + 1][h] if t < parts - 1 else pltpu.roll(v[x][0][h], SUB - 1, 0)
        total = total - coef_ref[2, x, t, h] * above
        if t > 0:
            total = total - coef_ref[2, x, t - 1, h] * v[x][t - 1][h]
        else:
            total = total - coef_ref[5, x, 0, h] * pltpu.roll(v[x][parts - 1][h], 1, 0)
        total = total - coef_ref[3, x, t, h] * front[h]
        result.append(total - coef_ref[4, x, t, h] * back[h])
    return result


def pairs_of(members):
    return [(a, b) for a in range(members) for b in range(a, members)]


def interior_kernel(k, pot_ref, kin_ref, orb_ref, body_ref, seam_ref, sums_ref, coef_ref, coef_ring, ring):
    members, rows_x, blocks_z = body_ref.shape[:3]
    rows_y = orb_ref.shape[2]
    parts = rows_y // SUB
    row, lane = iotas()
    upper = row < DEGREE
    own_coefficients(pot_ref, kin_ref, coef_ref, coef_ring, lane)
    for m in range(members):
        pair, half = m // 2, m % 2
        for x in range(rows_x):
            for h in range(blocks_z):
                ring[half, x, h] = orb_ref[k * members + m, x, :, cut(h)]
        v = [ring_tiles(ring.at[half], (x,), parts) for x in range(rows_x)]
        previous = None
        for step in range(DEGREE):
            for x in range(rows_x):
                for h in range(blocks_z):
                    for side in range(2):
                        for depth_in in range(2):
                            y = step + depth_in if side == 0 else rows_y - 1 - step - depth_in
                            place = DEGREE * half + (DEGREE - 1 if side == 0 else 0)
                            value = v[x][y % parts][h][y // parts : y // parts + 1]
                            seam_ref[side, pair, step, depth_in, x, h, place : place + 1, :] = value
            fresh = []
            for x in range(rows_x):
                rows = []
                for t in range(parts):
                    image = apply_own(coef_ref, v, x, t, lane)
                    if step == 0:
                        rows.append([0.5 * i for i in image])
                    else:
                        rows.append([i - p for i, p in zip(image, previous[x][t])])
                fresh.append(rows)
            previous, v = v, fresh
        for x in range(rows_x):
            for t in range(parts):
                for h in range(blocks_z):
                    ring[half, x, h, pl.ds(t, SUB, stride=parts), :] = v[x][t][h]
        for x in range(rows_x):
            for h in range(blocks_z):
                body_ref[m, x, h] = jnp.where(upper, ring[half, x, h, rows_y - SUB :], ring[half, x, h, 0:SUB])
    pairs = pairs_of(members)
    sums = [jnp.zeros((SUB, LANES), jnp.float32) for _ in pairs]
    for x in range(rows_x):
        for h in range(blocks_z):
            f = [body_ref[a, x, h] for a in range(members)]
            for i, (a, b) in enumerate(pairs):
                sums[i] = sums[i] + f[a] * f[b]
    for i, value in enumerate(sums):
        sums_ref[i] = value


def windows_kernel(second, odd_ref, pot_ref, kin_ref, halo_ref, coef_ref):
    rows_x, rows_y, depth = pot_ref.shape
    side = odd_ref[0] if second else 1 - odd_ref[0]
    top = side == 0
    row, lane = iotas()
    upper = row < DEGREE
    blocks_z = depth // LANES
    unit = 1.0 / HALF_WIDTH

    def window(tile, start):
        low = pltpu.roll(tile, lax.rem(SUB - start, SUB), 0)
        high = pltpu.roll(tile, lax.rem(SUB + DEGREE - start, SUB), 0)
        return jnp.where(upper, low, high)

    def field(c, x, h):
        own_ref = pot_ref if c == 0 else kin_ref.at[c - 1]
        halo = halo_ref[c // 2, x, :, cut(h)]
        head, tail = own_ref[x, 0:SUB, cut(h)], own_ref[x, rows_y - SUB :, cut(h)]
        before = pltpu.roll(halo, DEGREE, 0) if c % 2 else halo
        after = pltpu.roll(halo, 1 if c % 2 else DEGREE + 1, 0)
        above = jnp.where(upper, before, pltpu.roll(head, DEGREE, 0))
        below = jnp.where(row < DEGREE + 1, pltpu.roll(tail, DEGREE + 1, 0), after)
        return jnp.where(top, above, below)

    tiles = [[[field(c, x, h) for h in range(blocks_z)] for x in range(rows_x)] for c in range(4)]
    for step in range(DEGREE):
        start = jnp.where(top, step + 1, DEGREE - step)
        kx = [[window(tiles[1][x][h], start) for h in range(blocks_z)] for x in range(rows_x)]
        for x in range(rows_x):
            kz = [window(tiles[3][x][h], start) for h in range(blocks_z)]
            kzm = behind(kz, lane)
            for h in range(blocks_z):
                pot = window(tiles[0][x][h], start)
                ky = window(tiles[2][x][h], start)
                kym = window(tiles[2][x][h], start - 1)
                total = kx[x][h] + kx[(x - 1) % rows_x][h] + ky + kym + kz[h] + kzm[h]
                coef_ref[step, 0, x, h] = unit * total + (2.0 * unit) * (pot - CENTRE)
                coef_ref[step, 1, x, h] = unit * kx[x][h]
                coef_ref[step, 2, x, h] = unit * jnp.where(top, ky, kym)
                coef_ref[step, 3, x, h] = unit * jnp.where(top, kym, ky)
                coef_ref[step, 4, x, h] = unit * kz[h]
                coef_ref[step, 5, x, h] = unit * kzm[h]


def run_side(side, pair, w, seam_ref, coef_ref, lane, mark):
    rows_x, blocks_z = len(w), len(w[0])
    turn = jnp.where(side == 0, SUB - 1, 1)
    last = None
    for step in range(DEGREE):
        seam = seam_ref.at[side, pair, step]
        coef = coef_ref.at[step]
        centre, inner = [], []
        for x in range(rows_x):
            centre.append([jnp.where(mark, seam[0, x, h], pltpu.roll(w[x][h], turn, 0)) for h in range(blocks_z)])
            inner.append([jnp.where(mark, seam[1, x, h], pltpu.roll(centre[x][h], turn, 0)) for h in range(blocks_z)])
        fresh = []
        for x in range(rows_x):
            up_x, down_x = (x + 1) % rows_x, (x - 1) % rows_x
            front, back = ahead(centre[x], lane), behind(centre[x], lane)
            line = []
            for h in range(blocks_z):
                total = coef[0, x, h] * centre[x][h]
                total = total - coef[1, x, h] * centre[up_x][h]
                total = total - coef[1, down_x, h] * centre[down_x][h]
                total = total - coef[2, x, h] * inner[x][h]
                total = total - coef[3, x, h] * w[x][h]
                total = total - coef[4, x, h] * front[h]
                total = total - coef[5, x, h] * back[h]
                line.append(0.5 * total if step == 0 else total - last[x][h])
            fresh.append(line)
        last, w = inner, fresh
    return w


def edge_kernel(start, odd_ref, halo_ref, coef_ref, seam_ref, edge_ref):
    pairs, rows_x, blocks_z = edge_ref.shape[:3]
    row, lane = iotas()
    side = odd_ref[0]
    mark = row % DEGREE == jnp.where(side == 0, DEGREE - 1, 0)
    for pair in range(pairs):
        w = [[halo_ref[start + pair, x, :, cut(h)] for h in range(blocks_z)] for x in range(rows_x)]
        w = run_side(side, pair, w, seam_ref, coef_ref, lane, mark)
        for x in range(rows_x):
            for h in range(blocks_z):
                edge_ref[pair, x, h] = w[x][h]


def merge(first, second, place, odd, upper, edge_ref):
    for x in range(len(first)):
        for h in range(len(first[x])):
            a, b = first[x][h], second[x][h]
            top, bottom = jnp.where(odd, a, b), jnp.where(odd, b, a)
            edge_ref[place, x, h] = jnp.where(upper, top, pltpu.roll(bottom, DEGREE, 0))
            edge_ref[place + 1, x, h] = jnp.where(upper, pltpu.roll(top, DEGREE, 0), bottom)


def finish_kernel(start, odd_ref, halo_ref, coef_ref, seam_ref, sums_ref, second_ref, edge_ref, gram_ref):
    members, rows_x, blocks_z = edge_ref.shape[:3]
    row, lane = iotas()
    upper = row < DEGREE
    odd, side = odd_ref[0] == 1, 1 - odd_ref[0]
    mark = row % DEGREE == jnp.where(side == 0, DEGREE - 1, 0)
    for pair in range(members // 2):
        w = [[halo_ref[start + pair, x, :, cut(h)] for h in range(blocks_z)] for x in range(rows_x)]
        w = run_side(side, pair, w, seam_ref, coef_ref, lane, mark)
        second = [[second_ref[pair, x, h] for h in range(blocks_z)] for x in range(rows_x)]
        merge(w, second, 2 * pair, odd, upper, edge_ref)
    pairs = pairs_of(members)
    sums = [sums_ref[i] for i in range(len(pairs))]
    for x in range(rows_x):
        for h in range(blocks_z):
            f = [edge_ref[a, x, h] for a in range(members)]
            for i, (a, b) in enumerate(pairs):
                sums[i] = sums[i] + f[a] * f[b]
    at = {pair: jnp.sum(s, axis=0, keepdims=True) for pair, s in zip(pairs, sums)}
    column_of = lax.broadcasted_iota(jnp.int32, (members, members), 1)
    gram = jnp.zeros((members, members), jnp.float32)
    for a in range(members):
        column = jnp.concatenate([at[min(a, b), max(a, b)] for b in range(members)], 0)
        gram = jnp.where(column_of == a, jnp.sum(column, axis=1, keepdims=True), gram)
    gram_ref[...] = gram


def assemble_kernel(*refs):
    out_ref = refs[-1]
    rows_x, rows_y, depth = out_ref.shape[1:]
    row, _ = iotas()
    upper = row < DEGREE
    i = 0
    for body_ref, edge_ref in zip(refs[:-1:2], refs[1:-1:2]):
        for a in range(edge_ref.shape[0]):
            for x in range(rows_x):
                for h in range(depth // LANES):
                    body, edge = body_ref[a, x, h], edge_ref[a, x, h]
                    out_ref[i, x, 0:SUB, cut(h)] = jnp.where(upper, edge, body)
                    out_ref[i, x, rows_y - SUB :, cut(h)] = jnp.where(upper, body, edge)
            i += 1


def density_kernel(gram_ref, occ_ref, *refs):
    body_refs, edge_refs, out_ref = refs[:-1:2], refs[1:-1:2], refs[-1]
    rows_x, rows_y, depth = out_ref.shape
    blocks, members, _ = gram_ref.shape
    row, _ = iotas()
    upper = row < DEGREE
    down = lax.broadcasted_iota(jnp.int32, (members, members), 0)
    along = lax.broadcasted_iota(jnp.int32, (members, members), 1)
    w = []
    for k in range(blocks):
        ratio = jnp.broadcast_to(occ_ref[k : k + 1, :], (members, members)) / (gram_ref[k] + EPSILON)
        column = jnp.sum(jnp.where(down == along, ratio, 0.0), axis=1, keepdims=True)
        w += [jnp.broadcast_to(column[a : a + 1, :], (SUB, LANES)) for a in range(members)]
    for x in range(rows_x):
        for h in range(depth // LANES):
            body = edge = None
            for i in range(blocks * members):
                k, a = divmod(i, members)
                f, g = body_refs[k][a, x, h], edge_refs[k][a, x, h]
                f, g = w[i] * (f * f), w[i] * (g * g)
                body, edge = (f, g) if body is None else (body + f, edge + g)
            out_ref[x, 0:SUB, cut(h)] = jnp.where(upper, edge, body)
            out_ref[x, rows_y - SUB :, cut(h)] = jnp.where(upper, body, edge)


def vmem():
    return pl.BlockSpec(memory_space=pltpu.VMEM)


def smem():
    return pl.BlockSpec(memory_space=pltpu.SMEM)


def anywhere():
    return pl.BlockSpec(memory_space=pltpu.HBM)


def call(kernel, operands, outs, scratch=(), specs=None, place=jax.ShapeDtypeStruct, limit=8):
    shapes = tuple(place(shape, jnp.float32) for shape in outs)
    return pl.pallas_call(
        kernel,
        out_shape=shapes,
        in_specs=[vmem() for _ in operands] if specs is None else specs,
        out_specs=tuple(vmem() for _ in outs),
        scratch_shapes=[pltpu.VMEM(shape, jnp.float32) if isinstance(shape, tuple) else shape for shape in scratch],
        compiler_params=pltpu.CompilerParams(vmem_limit_bytes=limit * 1024 * 1024),
    )(*operands)


def fast_body(orbitals, potential, kinetic, occupations):
    blocks, members, _, rows_x, rows_y, depth = orbitals.shape
    count = blocks * members
    domains = lax.axis_size("grid")
    position = lax.axis_index("grid")
    parts = rows_y // SUB
    blocks_z = depth // LANES
    tile = (SUB, LANES)
    band = lax.axis_index("band")
    bands = lax.axis_size("band")
    odd = lax.rem(position, 2).astype(jnp.int32).reshape(1)

    pairs_a = [(i, i ^ 1) for i in range(domains)]
    pairs_b = [(i, (i + 1) % domains if i % 2 else (i - 1) % domains) for i in range(domains)]
    half = members // 2
    *halos, pot, kin, fields = call(
        functools.partial(pack_kernel, blocks),
        (
            odd,
            pltpu.with_memory_space_constraint(potential[0], pltpu.HBM),
            pltpu.with_memory_space_constraint(kinetic[:, 0], pltpu.HBM),
            pltpu.with_memory_space_constraint(orbitals.reshape(count, rows_x, rows_y, depth), pltpu.HBM),
        ),
        [(size, rows_x, SUB, depth) for size in [2 + half] + [half] * (blocks - 1) + [2 + count // 2]]
        + [(rows_x, rows_y, depth), (3, rows_x, rows_y, depth), (count, rows_x, rows_y, depth)],
        [pltpu.SemaphoreType.DMA((2 + blocks,))],
        specs=[smem()] + [anywhere()] * 3,
        place=pltpu.VMEM,
    )
    halos_a = []
    for k in range(blocks):
        halos_a.append(lax.ppermute(halos[k], "grid", pairs_a))
    halo_b = lax.ppermute(halos[blocks], "grid", pairs_b)

    inner = [
        call(
            functools.partial(interior_kernel, k),
            (pot, kin, fields),
            [
                (members, rows_x, blocks_z) + tile,
                (2, half, DEGREE, 2, rows_x, blocks_z) + tile,
                (len(pairs_of(members)),) + tile,
            ],
            [
                (6, rows_x, parts, blocks_z) + tile,
                (4, rows_x, blocks_z, rows_y, LANES),
                (2, rows_x, blocks_z, rows_y, LANES),
            ],
        )
        for k in range(blocks)
    ]
    coef_shape = (DEGREE, 6, rows_x, blocks_z) + tile
    (coef_a,) = call(
        functools.partial(windows_kernel, 0), (odd, pot, kin, halos_a[0]), [coef_shape], specs=[smem()] + [vmem()] * 3
    )
    (coef_b,) = call(
        functools.partial(windows_kernel, 1), (odd, pot, kin, halo_b), [coef_shape], specs=[smem()] + [vmem()] * 3
    )
    rows, grams = [], []
    for k in range(blocks):
        body, seam, sums = inner[k]
        (second,) = call(
            functools.partial(edge_kernel, 2 + k * half),
            (odd, halo_b, coef_b, seam),
            [(half, rows_x, blocks_z) + tile],
            specs=[smem()] + [vmem()] * 3,
        )
        edge, gram = call(
            functools.partial(finish_kernel, 0 if k else 2),
            (odd, halos_a[k], coef_a, seam, sums, second),
            [(members, rows_x, blocks_z) + tile, (members, members)],
            specs=[smem()] + [vmem()] * 5,
        )
        rows += [body, edge]
        grams.append(gram)
    gram = jnp.stack(grams)

    cells = rows_x * rows_y * depth * domains
    gram = gram * (1.0 / cells)
    bit = 1
    while bit < domains:
        gram = gram + swapped(gram, "grid", bit)
        bit *= 2

    (filtered,) = call(assemble_kernel, rows, [fields.shape])
    (partial_value,) = call(density_kernel, (gram, occupations, *rows), [pot.shape])

    share = rows_y // bands
    value = partial_value.reshape(rows_x, bands, share, depth)
    bit = 1
    width = bands
    while bit < bands:
        value = value.reshape(rows_x, width // 2, 2, share, depth)
        mine = (band // bit) % 2
        keep = lax.dynamic_index_in_dim(value, mine, 2, False)
        send = lax.dynamic_index_in_dim(value, 1 - mine, 2, False)
        value = keep + swapped(send, "band", bit)
        bit *= 2
        width //= 2
    density = value.reshape(1, rows_x, share, depth)
    return filtered.reshape(orbitals.shape), gram, density


def extend(field, width, across):
    lower = shifted(field[..., -width:, :, :], "grid", across)
    upper = shifted(field[..., :width, :, :], "grid", -across)
    widened = jnp.concatenate([lower, field, upper], -3)
    column = lax.axis_index("grid") % across
    left_plain = shifted(widened[..., :, -width:, :], "grid", 1)
    left_wrap = shifted(widened[..., :, -width:, :], "grid", -(across - 1))
    left = jnp.where(column == 0, left_wrap, left_plain)
    right_plain = shifted(widened[..., :, :width, :], "grid", -1)
    right_wrap = shifted(widened[..., :, :width, :], "grid", across - 1)
    right = jnp.where(column == across - 1, right_wrap, right_plain)
    return jnp.concatenate([left, widened, right], -2)


def hamilton(field, coeffs):
    inner = field[..., 1:-1, 1:-1, :]
    kin_x = coeffs[1]
    total = kin_x[1:-1, 1:-1] * (inner - field[..., 2:, 1:-1, :])
    total = total + kin_x[:-2, 1:-1] * (inner - field[..., :-2, 1:-1, :])
    kin_y = coeffs[2]
    total = total + kin_y[1:-1, 1:-1] * (inner - field[..., 1:-1, 2:, :])
    total = total + kin_y[1:-1, :-2] * (inner - field[..., 1:-1, :-2, :])
    kin_z = coeffs[3, 1:-1, 1:-1]
    total = total + kin_z * (inner - jnp.roll(inner, -1, -1))
    total = total + jnp.roll(kin_z, 1, -1) * (inner - jnp.roll(inner, 1, -1))
    return 0.5 * total + coeffs[0, 1:-1, 1:-1] * inner


def general_body(across, orbitals, potential, kinetic, occupations):
    blocks = orbitals.shape[0]
    members = orbitals.shape[1]
    rows_x = orbitals.shape[3]
    rows_y = orbitals.shape[4]
    coeffs = jnp.concatenate([potential, kinetic[:, 0]], 0)
    current = orbitals[:, :, 0]
    previous = current
    coeff_ext = None
    for degree_step in range(DEGREE):
        if degree_step == 0:
            stacked = jnp.concatenate(
                [coeffs, current.reshape((blocks * members,) + current.shape[2:])], 0
            )
            wide = extend(stacked, 1, across)
            coeff_ext = wide[:4]
            extended = wide[4:].reshape((blocks, members) + wide.shape[1:])
        else:
            extended = extend(current, 1, across)
        image = hamilton(extended, coeff_ext)
        inner = extended[..., 1:-1, 1:-1, :]
        if degree_step == 0:
            fresh = (image - CENTRE * inner) / HALF_WIDTH
        else:
            fresh = 2.0 / HALF_WIDTH * (image - CENTRE * inner) - previous
        previous = current
        current = fresh
    cells = rows_x * rows_y * orbitals.shape[5] * lax.axis_size("grid")
    flat = current.reshape(blocks, members, -1)
    local_gram = jnp.einsum("kbx,kcx->kbc", flat, flat, precision=lax.Precision.HIGHEST) / cells
    gram = lax.psum(local_gram, "grid")
    diagonal = jnp.diagonal(gram, axis1=1, axis2=2)
    weight = occupations / (diagonal + EPSILON)
    partial_value = jnp.einsum(
        "kb,kbxyz->xyz", weight, current * current, precision=lax.Precision.HIGHEST
    )
    density = lax.psum_scatter(partial_value[None], "band", scatter_dimension=2, tiled=True)
    return (current[:, :, None], gram, density)


def solution(mesh):
    domains = mesh.shape["grid"]
    across = min(domains, 8)
    even = all(size > 1 and size & (size - 1) == 0 for size in mesh.shape.values())
    fast = domains == across and even
    whole = fast_body if fast else functools.partial(general_body, across)

    placed = (
        P("band", None, "grid", None, None, None),
        P("grid", None, None, None),
        P(None, "grid", None, None, None),
        P("band", None),
    )
    return jax.shard_map(
        whole,
        mesh=mesh,
        in_specs=placed,
        out_specs=(
            P("band", None, "grid", None, None, None),
            P("band", None, None),
            P("grid", None, "band", None),
        ),
        check_vma=False,
    )
```

```python
import functools

import jax
import jax.numpy as jnp
from jax import lax
from jax.experimental import pallas as pl
from jax.experimental.pallas import tpu as pltpu
from jax.sharding import PartitionSpec as P


DEGREE = 4

CENTRE = 6.0
HALF_WIDTH = 4.0
EPSILON = 1e-06
SUB = 8
LANES = 128


def shifted(value, axis, steps):
    count = lax.axis_size(axis)
    pairs = [(source, (source + steps) % count) for source in range(count)]
    return lax.ppermute(value, axis, pairs)


def swapped(value, axis, bit):
    count = lax.axis_size(axis)
    return lax.ppermute(value, axis, [(i, i ^ bit) for i in range(count)])


def cut(h):
    return slice(LANES * h, LANES * (h + 1))


def iotas():
    return tuple(lax.broadcasted_iota(jnp.int32, (SUB, LANES), axis) for axis in range(2))


def ahead(line, lane):
    turned = [pltpu.roll(block, LANES - 1, 1) for block in line]
    return [jnp.where(lane == LANES - 1, turned[(h + 1) % len(line)], turned[h]) for h in range(len(line))]


def behind(line, lane):
    turned = [pltpu.roll(block, 1, 1) for block in line]
    return [jnp.where(lane == 0, turned[h - 1], turned[h]) for h in range(len(line))]


def pack_kernel(blocks, odd_ref, core_ref, pot_any, kin_any, orb_any, *refs):
    a_refs, b_refs = refs[:blocks], refs[blocks : 2 * blocks]
    pot_ref, kin_ref, orb_ref, arrivals = refs[2 * blocks :]
    count, rows_x, rows_y, depth = orb_ref.shape
    odd, core = odd_ref[0] == 1, core_ref[0] == 1
    row, _ = iotas()
    upper = row < DEGREE
    size = count // blocks
    loads = [pltpu.make_async_copy(pot_any, pot_ref, arrivals.at[0]), pltpu.make_async_copy(kin_any, kin_ref, arrivals.at[1])]
    for k in range(blocks):
        part = pl.ds(k * size, size)
        loads.append(pltpu.make_async_copy(orb_any.at[part], orb_ref.at[part], arrivals.at[2 + k]))
    for load in loads:
        load.start()

    def edges(one, two, x, h):
        tail = slice(rows_y - SUB, rows_y)
        first = jnp.where(upper, one[x, 0:SUB, cut(h)], pltpu.roll(two[x, 0:SUB, cut(h)], DEGREE, 0))
        last = jnp.where(upper, pltpu.roll(one[x, tail, cut(h)], DEGREE, 0), two[x, tail, cut(h)])
        return jnp.where(odd, first, last), jnp.where(odd, last, first)

    places = [(x, h) for x in range(rows_x) for h in range(depth // LANES)]
    loads[0].wait()
    loads[1].wait()
    for x, h in places:
        low_a, low_b = edges(pot_ref, kin_ref.at[0], x, h)
        high_a, high_b = edges(kin_ref.at[1], kin_ref.at[2], x, h)
        a_refs[0][0, x, :, cut(h)] = low_a
        a_refs[0][1, x, :, cut(h)] = high_a
        b_refs[0][0, x, :, cut(h)] = jnp.where(core, high_b, low_b)
    for k in range(blocks):
        loads[2 + k].wait()
        for p in range(size // 2):
            m = k * size + 2 * p
            for x, h in places:
                a, b = edges(orb_ref.at[m], orb_ref.at[m + 1], x, h)
                a_refs[k][(0 if k else 2) + p, x, :, cut(h)] = a
                b_refs[k][(0 if k else 1) + p, x, :, cut(h)] = b


def ring_tiles(ref, index, parts):
    return [
        [ref[index + (h, pl.ds(t, SUB, stride=parts), slice(None))] for h in range(ref.shape[-3])]
        for t in range(parts)
    ]


def own_coefficients(pot_ref, kin_ref, coef_ref, ring, lane):
    rows_x, rows_y, depth = pot_ref.shape
    parts = rows_y // SUB
    unit = 1.0 / HALF_WIDTH
    for x in range(rows_x):
        for c in range(4):
            own_ref = pot_ref if c == 0 else kin_ref.at[c - 1]
            for h in range(depth // LANES):
                ring[c, x, h] = own_ref[x, :, cut(h)]
    for x in range(rows_x):
        before = (x - 1) % rows_x
        pot = ring_tiles(ring, (0, x), parts)
        kx = ring_tiles(ring, (1, x), parts)
        kxm = ring_tiles(ring, (1, before), parts)
        ky = ring_tiles(ring, (2, x), parts)
        kz = ring_tiles(ring, (3, x), parts)
        for t in range(parts):
            kzm = behind(kz[t], lane)
            for h in range(depth // LANES):
                kym = ky[t - 1][h] if t > 0 else pltpu.roll(ky[parts - 1][h], 1, 0)
                total = kx[t][h] + kxm[t][h] + ky[t][h] + kym + kz[t][h] + kzm[h]
                coef_ref[0, x, t, h] = unit * total + (2.0 * unit) * (pot[t][h] - CENTRE)
                coef_ref[1, x, t, h] = unit * kx[t][h]
                coef_ref[2, x, t, h] = unit * ky[t][h]
                coef_ref[3, x, t, h] = unit * kz[t][h]
                coef_ref[4, x, t, h] = unit * kzm[h]
                if t == 0:
                    coef_ref[5, x, 0, h] = unit * kym


def apply_own(coef_ref, v, x, t, lane):
    rows_x, parts = len(v), len(v[0])
    up_x, down_x = (x + 1) % rows_x, (x - 1) % rows_x
    own = v[x][t]
    front, back = ahead(own, lane), behind(own, lane)
    result = []
    for h in range(len(own)):
        total = coef_ref[0, x, t, h] * own[h]
        total = total - coef_ref[1, x, t, h] * v[up_x][t][h]
        total = total - coef_ref[1, down_x, t, h] * v[down_x][t][h]
        above = v[x][t + 1][h] if t < parts - 1 else pltpu.roll(v[x][0][h], SUB - 1, 0)
        total = total - coef_ref[2, x, t, h] * above
        if t > 0:
            total = total - coef_ref[2, x, t - 1, h] * v[x][t - 1][h]
        else:
            total = total - coef_ref[5, x, 0, h] * pltpu.roll(v[x][parts - 1][h], 1, 0)
        total = total - coef_ref[3, x, t, h] * front[h]
        result.append(total - coef_ref[4, x, t, h] * back[h])
    return result


def pairs_of(members):
    return [(a, b) for a in range(members) for b in range(a, members)]


def interior_kernel(k, pot_ref, kin_ref, orb_ref, body_ref, seam_ref, sums_ref, coef_ref, coef_ring, ring):
    members, rows_x, blocks_z = body_ref.shape[:3]
    rows_y = orb_ref.shape[2]
    parts = rows_y // SUB
    row, lane = iotas()
    upper = row < DEGREE
    own_coefficients(pot_ref, kin_ref, coef_ref, coef_ring, lane)
    for m in range(members):
        pair, half = m // 2, m % 2
        for x in range(rows_x):
            for h in range(blocks_z):
                ring[half, x, h] = orb_ref[k * members + m, x, :, cut(h)]
        v = [ring_tiles(ring.at[half], (x,), parts) for x in range(rows_x)]
        previous = None
        for step in range(DEGREE):
            for x in range(rows_x):
                for h in range(blocks_z):
                    for side in range(2):
                        for depth_in in range(2):
                            y = step + depth_in if side == 0 else rows_y - 1 - step - depth_in
                            place = DEGREE * half + (DEGREE - 1 if side == 0 else 0)
                            value = v[x][y % parts][h][y // parts : y // parts + 1]
                            seam_ref[side, pair, step, depth_in, x, h, place : place + 1, :] = value
            fresh = []
            for x in range(rows_x):
                rows = []
                for t in range(parts):
                    image = apply_own(coef_ref, v, x, t, lane)
                    if step == 0:
                        rows.append([0.5 * i for i in image])
                    else:
                        rows.append([i - p for i, p in zip(image, previous[x][t])])
                fresh.append(rows)
            previous, v = v, fresh
        for x in range(rows_x):
            for t in range(parts):
                for h in range(blocks_z):
                    ring[half, x, h, pl.ds(t, SUB, stride=parts), :] = v[x][t][h]
        for x in range(rows_x):
            for h in range(blocks_z):
                body_ref[m, x, h] = jnp.where(upper, ring[half, x, h, rows_y - SUB :], ring[half, x, h, 0:SUB])
    pairs = pairs_of(members)
    sums = [jnp.zeros((SUB, LANES), jnp.float32) for _ in pairs]
    for x in range(rows_x):
        for h in range(blocks_z):
            f = [body_ref[a, x, h] for a in range(members)]
            for i, (a, b) in enumerate(pairs):
                sums[i] = sums[i] + f[a] * f[b]
    for i, value in enumerate(sums):
        sums_ref[i] = value


def windows_kernel(second, odd_ref, core_ref, pot_ref, kin_ref, *refs):
    halo_refs, coef_ref = refs[:-1], refs[-1]
    rows_x, rows_y, depth = pot_ref.shape
    core = core_ref[0] == 1
    side = odd_ref[0] if second else 1 - odd_ref[0]
    top = side == 0
    row, lane = iotas()
    upper = row < DEGREE
    blocks_z = depth // LANES
    unit = 1.0 / HALF_WIDTH

    def window(tile, start):
        low = pltpu.roll(tile, lax.rem(SUB - start, SUB), 0)
        high = pltpu.roll(tile, lax.rem(SUB + DEGREE - start, SUB), 0)
        return jnp.where(upper, low, high)

    def field(c, x, h):
        own_ref = pot_ref if c == 0 else kin_ref.at[c - 1]
        if second:
            mine = core if c // 2 else jnp.logical_not(core)
            halo = jnp.where(mine, halo_refs[0][0, x, :, cut(h)], halo_refs[1][0, x, :, cut(h)])
        else:
            halo = halo_refs[0][c // 2, x, :, cut(h)]
        head, tail = own_ref[x, 0:SUB, cut(h)], own_ref[x, rows_y - SUB :, cut(h)]
        before = pltpu.roll(halo, DEGREE, 0) if c % 2 else halo
        after = pltpu.roll(halo, 1 if c % 2 else DEGREE + 1, 0)
        above = jnp.where(upper, before, pltpu.roll(head, DEGREE, 0))
        below = jnp.where(row < DEGREE + 1, pltpu.roll(tail, DEGREE + 1, 0), after)
        return jnp.where(top, above, below)

    tiles = [[[field(c, x, h) for h in range(blocks_z)] for x in range(rows_x)] for c in range(4)]
    for step in range(DEGREE):
        start = jnp.where(top, step + 1, DEGREE - step)
        kx = [[window(tiles[1][x][h], start) for h in range(blocks_z)] for x in range(rows_x)]
        for x in range(rows_x):
            kz = [window(tiles[3][x][h], start) for h in range(blocks_z)]
            kzm = behind(kz, lane)
            for h in range(blocks_z):
                pot = window(tiles[0][x][h], start)
                ky = window(tiles[2][x][h], start)
                kym = window(tiles[2][x][h], start - 1)
                total = kx[x][h] + kx[(x - 1) % rows_x][h] + ky + kym + kz[h] + kzm[h]
                coef_ref[step, 0, x, h] = unit * total + (2.0 * unit) * (pot - CENTRE)
                coef_ref[step, 1, x, h] = unit * kx[x][h]
                coef_ref[step, 2, x, h] = unit * jnp.where(top, ky, kym)
                coef_ref[step, 3, x, h] = unit * jnp.where(top, kym, ky)
                coef_ref[step, 4, x, h] = unit * kz[h]
                coef_ref[step, 5, x, h] = unit * kzm[h]


def run_side(side, pair, w, seam_ref, coef_ref, lane, mark):
    rows_x, blocks_z = len(w), len(w[0])
    turn = jnp.where(side == 0, SUB - 1, 1)
    last = None
    for step in range(DEGREE):
        seam = seam_ref.at[side, pair, step]
        coef = coef_ref.at[step]
        centre, inner = [], []
        for x in range(rows_x):
            centre.append([jnp.where(mark, seam[0, x, h], pltpu.roll(w[x][h], turn, 0)) for h in range(blocks_z)])
            inner.append([jnp.where(mark, seam[1, x, h], pltpu.roll(centre[x][h], turn, 0)) for h in range(blocks_z)])
        fresh = []
        for x in range(rows_x):
            up_x, down_x = (x + 1) % rows_x, (x - 1) % rows_x
            front, back = ahead(centre[x], lane), behind(centre[x], lane)
            line = []
            for h in range(blocks_z):
                total = coef[0, x, h] * centre[x][h]
                total = total - coef[1, x, h] * centre[up_x][h]
                total = total - coef[1, down_x, h] * centre[down_x][h]
                total = total - coef[2, x, h] * inner[x][h]
                total = total - coef[3, x, h] * w[x][h]
                total = total - coef[4, x, h] * front[h]
                total = total - coef[5, x, h] * back[h]
                line.append(0.5 * total if step == 0 else total - last[x][h])
            fresh.append(line)
        last, w = inner, fresh
    return w


def edge_kernel(start, odd_ref, halo_ref, coef_ref, seam_ref, edge_ref):
    pairs, rows_x, blocks_z = edge_ref.shape[:3]
    row, lane = iotas()
    side = odd_ref[0]
    mark = row % DEGREE == jnp.where(side == 0, DEGREE - 1, 0)
    for pair in range(pairs):
        w = [[halo_ref[start + pair, x, :, cut(h)] for h in range(blocks_z)] for x in range(rows_x)]
        w = run_side(side, pair, w, seam_ref, coef_ref, lane, mark)
        for x in range(rows_x):
            for h in range(blocks_z):
                edge_ref[pair, x, h] = w[x][h]


def merge(first, second, place, odd, upper, edge_ref):
    for x in range(len(first)):
        for h in range(len(first[x])):
            a, b = first[x][h], second[x][h]
            top, bottom = jnp.where(odd, a, b), jnp.where(odd, b, a)
            edge_ref[place, x, h] = jnp.where(upper, top, pltpu.roll(bottom, DEGREE, 0))
            edge_ref[place + 1, x, h] = jnp.where(upper, pltpu.roll(top, DEGREE, 0), bottom)


def finish_kernel(start, odd_ref, halo_ref, coef_ref, seam_ref, sums_ref, second_ref, edge_ref, gram_ref):
    members, rows_x, blocks_z = edge_ref.shape[:3]
    row, lane = iotas()
    upper = row < DEGREE
    odd, side = odd_ref[0] == 1, 1 - odd_ref[0]
    mark = row % DEGREE == jnp.where(side == 0, DEGREE - 1, 0)
    for pair in range(members // 2):
        w = [[halo_ref[start + pair, x, :, cut(h)] for h in range(blocks_z)] for x in range(rows_x)]
        w = run_side(side, pair, w, seam_ref, coef_ref, lane, mark)
        second = [[second_ref[pair, x, h] for h in range(blocks_z)] for x in range(rows_x)]
        merge(w, second, 2 * pair, odd, upper, edge_ref)
    pairs = pairs_of(members)
    sums = [sums_ref[i] for i in range(len(pairs))]
    for x in range(rows_x):
        for h in range(blocks_z):
            f = [edge_ref[a, x, h] for a in range(members)]
            for i, (a, b) in enumerate(pairs):
                sums[i] = sums[i] + f[a] * f[b]
    at = {pair: jnp.sum(s, axis=0, keepdims=True) for pair, s in zip(pairs, sums)}
    column_of = lax.broadcasted_iota(jnp.int32, (members, members), 1)
    gram = jnp.zeros((members, members), jnp.float32)
    for a in range(members):
        column = jnp.concatenate([at[min(a, b), max(a, b)] for b in range(members)], 0)
        gram = jnp.where(column_of == a, jnp.sum(column, axis=1, keepdims=True), gram)
    gram_ref[...] = gram


def assemble_kernel(*refs):
    out_ref = refs[-1]
    rows_x, rows_y, depth = out_ref.shape[1:]
    row, _ = iotas()
    upper = row < DEGREE
    i = 0
    for body_ref, edge_ref in zip(refs[:-1:2], refs[1:-1:2]):
        for a in range(edge_ref.shape[0]):
            for x in range(rows_x):
                for h in range(depth // LANES):
                    body, edge = body_ref[a, x, h], edge_ref[a, x, h]
                    out_ref[i, x, 0:SUB, cut(h)] = jnp.where(upper, edge, body)
                    out_ref[i, x, rows_y - SUB :, cut(h)] = jnp.where(upper, body, edge)
            i += 1


def density_kernel(gram_ref, occ_ref, *refs):
    body_refs, edge_refs, out_ref = refs[:-1:2], refs[1:-1:2], refs[-1]
    rows_x, rows_y, depth = out_ref.shape
    blocks, members, _ = gram_ref.shape
    row, _ = iotas()
    upper = row < DEGREE
    down = lax.broadcasted_iota(jnp.int32, (members, members), 0)
    along = lax.broadcasted_iota(jnp.int32, (members, members), 1)
    w = []
    for k in range(blocks):
        ratio = jnp.broadcast_to(occ_ref[k : k + 1, :], (members, members)) / (gram_ref[k] + EPSILON)
        column = jnp.sum(jnp.where(down == along, ratio, 0.0), axis=1, keepdims=True)
        w += [jnp.broadcast_to(column[a : a + 1, :], (SUB, LANES)) for a in range(members)]
    for x in range(rows_x):
        for h in range(depth // LANES):
            body = edge = None
            for i in range(blocks * members):
                k, a = divmod(i, members)
                f, g = body_refs[k][a, x, h], edge_refs[k][a, x, h]
                f, g = w[i] * (f * f), w[i] * (g * g)
                body, edge = (f, g) if body is None else (body + f, edge + g)
            out_ref[x, 0:SUB, cut(h)] = jnp.where(upper, edge, body)
            out_ref[x, rows_y - SUB :, cut(h)] = jnp.where(upper, body, edge)


def vmem():
    return pl.BlockSpec(memory_space=pltpu.VMEM)


def smem():
    return pl.BlockSpec(memory_space=pltpu.SMEM)


def anywhere():
    return pl.BlockSpec(memory_space=pltpu.HBM)


def call(kernel, operands, outs, scratch=(), specs=None, place=jax.ShapeDtypeStruct, limit=8):
    shapes = tuple(place(shape, jnp.float32) for shape in outs)
    return pl.pallas_call(
        kernel,
        out_shape=shapes,
        in_specs=[vmem() for _ in operands] if specs is None else specs,
        out_specs=tuple(vmem() for _ in outs),
        scratch_shapes=[pltpu.VMEM(shape, jnp.float32) if isinstance(shape, tuple) else shape for shape in scratch],
        compiler_params=pltpu.CompilerParams(vmem_limit_bytes=limit * 1024 * 1024),
    )(*operands)


def fast_body(orbitals, potential, kinetic, occupations):
    blocks, members, _, rows_x, rows_y, depth = orbitals.shape
    count = blocks * members
    domains = lax.axis_size("grid")
    position = lax.axis_index("grid")
    parts = rows_y // SUB
    blocks_z = depth // LANES
    tile = (SUB, LANES)
    band = lax.axis_index("band")
    bands = lax.axis_size("band")
    odd = lax.rem(position, 2).astype(jnp.int32).reshape(1)
    core = lax.rem(band, 2).astype(jnp.int32).reshape(1)

    pairs_a = [(i, i ^ 1) for i in range(domains)]
    pairs_b = [(i, (i + 1) % domains if i % 2 else (i - 1) % domains) for i in range(domains)]
    half = members // 2
    *halos, pot, kin, fields = call(
        functools.partial(pack_kernel, blocks),
        (
            odd,
            core,
            pltpu.with_memory_space_constraint(potential[0], pltpu.HBM),
            pltpu.with_memory_space_constraint(kinetic[:, 0], pltpu.HBM),
            pltpu.with_memory_space_constraint(orbitals.reshape(count, rows_x, rows_y, depth), pltpu.HBM),
        ),
        [(size, rows_x, SUB, depth) for size in [2 + half] + [half] * (blocks - 1) + [1 + half] + [half] * (blocks - 1)]
        + [(rows_x, rows_y, depth), (3, rows_x, rows_y, depth), (count, rows_x, rows_y, depth)],
        [pltpu.SemaphoreType.DMA((2 + blocks,))],
        specs=[smem()] * 2 + [anywhere()] * 3,
        place=pltpu.VMEM,
    )
    halos_a = []
    for k in range(blocks):
        halos_a.append(lax.ppermute(halos[k], "grid", pairs_a))
    halos_b = []
    for k in range(blocks):
        halos_b.append(lax.ppermute(halos[blocks + k], "grid", pairs_b))
    other = swapped(halos_b[0][:1], "band", 1)

    inner = [
        call(
            functools.partial(interior_kernel, k),
            (pot, kin, fields),
            [
                (members, rows_x, blocks_z) + tile,
                (2, half, DEGREE, 2, rows_x, blocks_z) + tile,
                (len(pairs_of(members)),) + tile,
            ],
            [
                (6, rows_x, parts, blocks_z) + tile,
                (4, rows_x, blocks_z, rows_y, LANES),
                (2, rows_x, blocks_z, rows_y, LANES),
            ],
        )
        for k in range(blocks)
    ]
    coef_shape = (DEGREE, 6, rows_x, blocks_z) + tile
    (coef_a,) = call(
        functools.partial(windows_kernel, 0),
        (odd, core, pot, kin, halos_a[0]),
        [coef_shape],
        specs=[smem()] * 2 + [vmem()] * 3,
    )
    (coef_b,) = call(
        functools.partial(windows_kernel, 1),
        (odd, core, pot, kin, halos_b[0], other),
        [coef_shape],
        specs=[smem()] * 2 + [vmem()] * 4,
    )
    rows, grams = [], []
    for k in range(blocks):
        body, seam, sums = inner[k]
        (second,) = call(
            functools.partial(edge_kernel, 0 if k else 1),
            (odd, halos_b[k], coef_b, seam),
            [(half, rows_x, blocks_z) + tile],
            specs=[smem()] + [vmem()] * 3,
        )
        edge, gram = call(
            functools.partial(finish_kernel, 0 if k else 2),
            (odd, halos_a[k], coef_a, seam, sums, second),
            [(members, rows_x, blocks_z) + tile, (members, members)],
            specs=[smem()] + [vmem()] * 5,
        )
        rows += [body, edge]
        grams.append(gram)
    gram = jnp.stack(grams)

    cells = rows_x * rows_y * depth * domains
    gram = gram * (1.0 / cells)
    bit = 1
    while bit < domains:
        gram = gram + swapped(gram, "grid", bit)
        bit *= 2

    (filtered,) = call(assemble_kernel, rows, [fields.shape])
    (partial_value,) = call(density_kernel, (gram, occupations, *rows), [pot.shape])

    share = rows_y // bands
    value = partial_value.reshape(rows_x, bands, share, depth)
    bit = 1
    width = bands
    while bit < bands:
        value = value.reshape(rows_x, width // 2, 2, share, depth)
        mine = (band // bit) % 2
        keep = lax.dynamic_index_in_dim(value, mine, 2, False)
        send = lax.dynamic_index_in_dim(value, 1 - mine, 2, False)
        value = keep + swapped(send, "band", bit)
        bit *= 2
        width //= 2
    density = value.reshape(1, rows_x, share, depth)
    return filtered.reshape(orbitals.shape), gram, density


def extend(field, width, across):
    lower = shifted(field[..., -width:, :, :], "grid", across)
    upper = shifted(field[..., :width, :, :], "grid", -across)
    widened = jnp.concatenate([lower, field, upper], -3)
    column = lax.axis_index("grid") % across
    left_plain = shifted(widened[..., :, -width:, :], "grid", 1)
    left_wrap = shifted(widened[..., :, -width:, :], "grid", -(across - 1))
    left = jnp.where(column == 0, left_wrap, left_plain)
    right_plain = shifted(widened[..., :, :width, :], "grid", -1)
    right_wrap = shifted(widened[..., :, :width, :], "grid", across - 1)
    right = jnp.where(column == across - 1, right_wrap, right_plain)
    return jnp.concatenate([left, widened, right], -2)


def hamilton(field, coeffs):
    inner = field[..., 1:-1, 1:-1, :]
    kin_x = coeffs[1]
    total = kin_x[1:-1, 1:-1] * (inner - field[..., 2:, 1:-1, :])
    total = total + kin_x[:-2, 1:-1] * (inner - field[..., :-2, 1:-1, :])
    kin_y = coeffs[2]
    total = total + kin_y[1:-1, 1:-1] * (inner - field[..., 1:-1, 2:, :])
    total = total + kin_y[1:-1, :-2] * (inner - field[..., 1:-1, :-2, :])
    kin_z = coeffs[3, 1:-1, 1:-1]
    total = total + kin_z * (inner - jnp.roll(inner, -1, -1))
    total = total + jnp.roll(kin_z, 1, -1) * (inner - jnp.roll(inner, 1, -1))
    return 0.5 * total + coeffs[0, 1:-1, 1:-1] * inner


def general_body(across, orbitals, potential, kinetic, occupations):
    blocks = orbitals.shape[0]
    members = orbitals.shape[1]
    rows_x = orbitals.shape[3]
    rows_y = orbitals.shape[4]
    coeffs = jnp.concatenate([potential, kinetic[:, 0]], 0)
    current = orbitals[:, :, 0]
    previous = current
    coeff_ext = None
    for degree_step in range(DEGREE):
        if degree_step == 0:
            stacked = jnp.concatenate(
                [coeffs, current.reshape((blocks * members,) + current.shape[2:])], 0
            )
            wide = extend(stacked, 1, across)
            coeff_ext = wide[:4]
            extended = wide[4:].reshape((blocks, members) + wide.shape[1:])
        else:
            extended = extend(current, 1, across)
        image = hamilton(extended, coeff_ext)
        inner = extended[..., 1:-1, 1:-1, :]
        if degree_step == 0:
            fresh = (image - CENTRE * inner) / HALF_WIDTH
        else:
            fresh = 2.0 / HALF_WIDTH * (image - CENTRE * inner) - previous
        previous = current
        current = fresh
    cells = rows_x * rows_y * orbitals.shape[5] * lax.axis_size("grid")
    flat = current.reshape(blocks, members, -1)
    local_gram = jnp.einsum("kbx,kcx->kbc", flat, flat, precision=lax.Precision.HIGHEST) / cells
    gram = lax.psum(local_gram, "grid")
    diagonal = jnp.diagonal(gram, axis1=1, axis2=2)
    weight = occupations / (diagonal + EPSILON)
    partial_value = jnp.einsum(
        "kb,kbxyz->xyz", weight, current * current, precision=lax.Precision.HIGHEST
    )
    density = lax.psum_scatter(partial_value[None], "band", scatter_dimension=2, tiled=True)
    return (current[:, :, None], gram, density)


def solution(mesh):
    domains = mesh.shape["grid"]
    across = min(domains, 8)
    even = all(size > 1 and size & (size - 1) == 0 for size in mesh.shape.values())
    fast = domains == across and even
    whole = fast_body if fast else functools.partial(general_body, across)

    placed = (
        P("band", None, "grid", None, None, None),
        P("grid", None, None, None),
        P(None, "grid", None, None, None),
        P("band", None),
    )
    return jax.shard_map(
        whole,
        mesh=mesh,
        in_specs=placed,
        out_specs=(
            P("band", None, "grid", None, None, None),
            P("band", None, None),
            P("grid", None, "band", None),
        ),
        check_vma=False,
    )
```

```python
import functools

import jax
import jax.numpy as jnp
from jax import lax
from jax.experimental import pallas as pl
from jax.experimental.pallas import tpu as pltpu
from jax.sharding import PartitionSpec as P


DEGREE = 4

CENTRE = 6.0
HALF_WIDTH = 4.0
EPSILON = 1e-06
SUB = 8
LANES = 128


def shifted(value, axis, steps):
    count = lax.axis_size(axis)
    pairs = [(source, (source + steps) % count) for source in range(count)]
    return lax.ppermute(value, axis, pairs)


def swapped(value, axis, bit):
    count = lax.axis_size(axis)
    return lax.ppermute(value, axis, [(i, i ^ bit) for i in range(count)])


def cut(h):
    return slice(LANES * h, LANES * (h + 1))


def iotas():
    return tuple(lax.broadcasted_iota(jnp.int32, (SUB, LANES), axis) for axis in range(2))


def ahead(line, lane):
    turned = [pltpu.roll(block, LANES - 1, 1) for block in line]
    return [jnp.where(lane == LANES - 1, turned[(h + 1) % len(line)], turned[h]) for h in range(len(line))]


def behind(line, lane):
    turned = [pltpu.roll(block, 1, 1) for block in line]
    return [jnp.where(lane == 0, turned[h - 1], turned[h]) for h in range(len(line))]


def field_edges(odd, one, two, x, h):
    rows_y = one.shape[-2]
    row, _ = iotas()
    upper = row < DEGREE
    tail = slice(rows_y - SUB, rows_y)
    first = jnp.where(upper, one[x, 0:SUB, cut(h)], pltpu.roll(two[x, 0:SUB, cut(h)], DEGREE, 0))
    last = jnp.where(upper, pltpu.roll(one[x, tail, cut(h)], DEGREE, 0), two[x, tail, cut(h)])
    return jnp.where(odd, first, last), jnp.where(odd, last, first)


def pack_kernel(odd_ref, core_ref, pot_any, kin_any, orb_any, a_ref, b_ref, pot_ref, kin_ref, orb_ref, arrivals):
    rows_x, _, depth = pot_ref.shape
    members = orb_ref.shape[0]
    odd, core = odd_ref[0] == 1, core_ref[0] == 1
    loads = [
        pltpu.make_async_copy(pot_any, pot_ref, arrivals.at[0]),
        pltpu.make_async_copy(kin_any, kin_ref, arrivals.at[1]),
        pltpu.make_async_copy(orb_any.at[pl.ds(0, members)], orb_ref, arrivals.at[2]),
    ]
    for load in loads:
        load.start()
    places = [(x, h) for x in range(rows_x) for h in range(depth // LANES)]
    loads[0].wait()
    loads[1].wait()
    for x, h in places:
        low_a, low_b = field_edges(odd, pot_ref, kin_ref.at[0], x, h)
        high_a, high_b = field_edges(odd, kin_ref.at[1], kin_ref.at[2], x, h)
        a_ref[0, x, :, cut(h)] = low_a
        a_ref[1, x, :, cut(h)] = high_a
        b_ref[0, x, :, cut(h)] = jnp.where(core, high_b, low_b)
    loads[2].wait()
    for p in range(members // 2):
        for x, h in places:
            a, b = field_edges(odd, orb_ref.at[2 * p], orb_ref.at[2 * p + 1], x, h)
            a_ref[2 + p, x, :, cut(h)] = a
            b_ref[1 + p, x, :, cut(h)] = b


def rest_kernel(k, odd_ref, orb_any, a_ref, b_ref, orb_ref, arrivals):
    members, rows_x, _, depth = orb_ref.shape
    odd = odd_ref[0] == 1
    load = pltpu.make_async_copy(orb_any.at[pl.ds(k * members, members)], orb_ref, arrivals.at[0])
    load.start()
    load.wait()
    for p in range(members // 2):
        for x in range(rows_x):
            for h in range(depth // LANES):
                a, b = field_edges(odd, orb_ref.at[2 * p], orb_ref.at[2 * p + 1], x, h)
                a_ref[p, x, :, cut(h)] = a
                b_ref[p, x, :, cut(h)] = b


def ring_tiles(ref, index, parts):
    return [
        [ref[index + (h, pl.ds(t, SUB, stride=parts), slice(None))] for h in range(ref.shape[-3])]
        for t in range(parts)
    ]


def own_coefficients(pot_ref, kin_ref, coef_ref, ring, lane):
    rows_x, rows_y, depth = pot_ref.shape
    parts = rows_y // SUB
    unit = 1.0 / HALF_WIDTH
    for x in range(rows_x):
        for c in range(4):
            own_ref = pot_ref if c == 0 else kin_ref.at[c - 1]
            for h in range(depth // LANES):
                ring[c, x, h] = own_ref[x, :, cut(h)]
    for x in range(rows_x):
        before = (x - 1) % rows_x
        pot = ring_tiles(ring, (0, x), parts)
        kx = ring_tiles(ring, (1, x), parts)
        kxm = ring_tiles(ring, (1, before), parts)
        ky = ring_tiles(ring, (2, x), parts)
        kz = ring_tiles(ring, (3, x), parts)
        for t in range(parts):
            kzm = behind(kz[t], lane)
            for h in range(depth // LANES):
                kym = ky[t - 1][h] if t > 0 else pltpu.roll(ky[parts - 1][h], 1, 0)
                total = kx[t][h] + kxm[t][h] + ky[t][h] + kym + kz[t][h] + kzm[h]
                coef_ref[0, x, t, h] = unit * total + (2.0 * unit) * (pot[t][h] - CENTRE)
                coef_ref[1, x, t, h] = unit * kx[t][h]
                coef_ref[2, x, t, h] = unit * ky[t][h]
                coef_ref[3, x, t, h] = unit * kz[t][h]
                coef_ref[4, x, t, h] = unit * kzm[h]
                if t == 0:
                    coef_ref[5, x, 0, h] = unit * kym


def apply_own(coef_ref, v, x, t, lane):
    rows_x, parts = len(v), len(v[0])
    up_x, down_x = (x + 1) % rows_x, (x - 1) % rows_x
    own = v[x][t]
    front, back = ahead(own, lane), behind(own, lane)
    result = []
    for h in range(len(own)):
        total = coef_ref[0, x, t, h] * own[h]
        total = total - coef_ref[1, x, t, h] * v[up_x][t][h]
        total = total - coef_ref[1, down_x, t, h] * v[down_x][t][h]
        above = v[x][t + 1][h] if t < parts - 1 else pltpu.roll(v[x][0][h], SUB - 1, 0)
        total = total - coef_ref[2, x, t, h] * above
        if t > 0:
            total = total - coef_ref[2, x, t - 1, h] * v[x][t - 1][h]
        else:
            total = total - coef_ref[5, x, 0, h] * pltpu.roll(v[x][parts - 1][h], 1, 0)
        total = total - coef_ref[3, x, t, h] * front[h]
        result.append(total - coef_ref[4, x, t, h] * back[h])
    return result


def pairs_of(members):
    return [(a, b) for a in range(members) for b in range(a, members)]


def interior_kernel(pot_ref, kin_ref, orb_ref, body_ref, seam_ref, sums_ref, coef_ref, coef_ring, ring):
    members, rows_x, blocks_z = body_ref.shape[:3]
    rows_y = orb_ref.shape[2]
    parts = rows_y // SUB
    row, lane = iotas()
    upper = row < DEGREE
    own_coefficients(pot_ref, kin_ref, coef_ref, coef_ring, lane)
    for m in range(members):
        pair, half = m // 2, m % 2
        for x in range(rows_x):
            for h in range(blocks_z):
                ring[half, x, h] = orb_ref[m, x, :, cut(h)]
        v = [ring_tiles(ring.at[half], (x,), parts) for x in range(rows_x)]
        previous = None
        for step in range(DEGREE):
            for x in range(rows_x):
                for h in range(blocks_z):
                    for side in range(2):
                        for depth_in in range(2):
                            y = step + depth_in if side == 0 else rows_y - 1 - step - depth_in
                            place = DEGREE * half + (DEGREE - 1 if side == 0 else 0)
                            value = v[x][y % parts][h][y // parts : y // parts + 1]
                            seam_ref[side, pair, step, depth_in, x, h, place : place + 1, :] = value
            fresh = []
            for x in range(rows_x):
                rows = []
                for t in range(parts):
                    image = apply_own(coef_ref, v, x, t, lane)
                    if step == 0:
                        rows.append([0.5 * i for i in image])
                    else:
                        rows.append([i - p for i, p in zip(image, previous[x][t])])
                fresh.append(rows)
            previous, v = v, fresh
        for x in range(rows_x):
            for t in range(parts):
                for h in range(blocks_z):
                    ring[half, x, h, pl.ds(t, SUB, stride=parts), :] = v[x][t][h]
        for x in range(rows_x):
            for h in range(blocks_z):
                body_ref[m, x, h] = jnp.where(upper, ring[half, x, h, rows_y - SUB :], ring[half, x, h, 0:SUB])
    pairs = pairs_of(members)
    sums = [jnp.zeros((SUB, LANES), jnp.float32) for _ in pairs]
    for x in range(rows_x):
        for h in range(blocks_z):
            f = [body_ref[a, x, h] for a in range(members)]
            for i, (a, b) in enumerate(pairs):
                sums[i] = sums[i] + f[a] * f[b]
    for i, value in enumerate(sums):
        sums_ref[i] = value


def windows_kernel(second, odd_ref, core_ref, pot_ref, kin_ref, *refs):
    halo_refs, coef_ref = refs[:-1], refs[-1]
    rows_x, rows_y, depth = pot_ref.shape
    core = core_ref[0] == 1
    side = odd_ref[0] if second else 1 - odd_ref[0]
    top = side == 0
    row, lane = iotas()
    upper = row < DEGREE
    blocks_z = depth // LANES
    unit = 1.0 / HALF_WIDTH

    def window(tile, start):
        low = pltpu.roll(tile, lax.rem(SUB - start, SUB), 0)
        high = pltpu.roll(tile, lax.rem(SUB + DEGREE - start, SUB), 0)
        return jnp.where(upper, low, high)

    def field(c, x, h):
        own_ref = pot_ref if c == 0 else kin_ref.at[c - 1]
        if second:
            mine = core if c // 2 else jnp.logical_not(core)
            halo = jnp.where(mine, halo_refs[0][0, x, :, cut(h)], halo_refs[1][0, x, :, cut(h)])
        else:
            halo = halo_refs[0][c // 2, x, :, cut(h)]
        head, tail = own_ref[x, 0:SUB, cut(h)], own_ref[x, rows_y - SUB :, cut(h)]
        before = pltpu.roll(halo, DEGREE, 0) if c % 2 else halo
        after = pltpu.roll(halo, 1 if c % 2 else DEGREE + 1, 0)
        above = jnp.where(upper, before, pltpu.roll(head, DEGREE, 0))
        below = jnp.where(row < DEGREE + 1, pltpu.roll(tail, DEGREE + 1, 0), after)
        return jnp.where(top, above, below)

    tiles = [[[field(c, x, h) for h in range(blocks_z)] for x in range(rows_x)] for c in range(4)]
    for step in range(DEGREE):
        start = jnp.where(top, step + 1, DEGREE - step)
        kx = [[window(tiles[1][x][h], start) for h in range(blocks_z)] for x in range(rows_x)]
        for x in range(rows_x):
            kz = [window(tiles[3][x][h], start) for h in range(blocks_z)]
            kzm = behind(kz, lane)
            for h in range(blocks_z):
                pot = window(tiles[0][x][h], start)
                ky = window(tiles[2][x][h], start)
                kym = window(tiles[2][x][h], start - 1)
                total = kx[x][h] + kx[(x - 1) % rows_x][h] + ky + kym + kz[h] + kzm[h]
                coef_ref[step, 0, x, h] = unit * total + (2.0 * unit) * (pot - CENTRE)
                coef_ref[step, 1, x, h] = unit * kx[x][h]
                coef_ref[step, 2, x, h] = unit * jnp.where(top, ky, kym)
                coef_ref[step, 3, x, h] = unit * jnp.where(top, kym, ky)
                coef_ref[step, 4, x, h] = unit * kz[h]
                coef_ref[step, 5, x, h] = unit * kzm[h]


def run_side(side, pair, w, seam_ref, coef_ref, lane, mark):
    rows_x, blocks_z = len(w), len(w[0])
    turn = jnp.where(side == 0, SUB - 1, 1)
    last = None
    for step in range(DEGREE):
        seam = seam_ref.at[side, pair, step]
        coef = coef_ref.at[step]
        centre, inner = [], []
        for x in range(rows_x):
            centre.append([jnp.where(mark, seam[0, x, h], pltpu.roll(w[x][h], turn, 0)) for h in range(blocks_z)])
            inner.append([jnp.where(mark, seam[1, x, h], pltpu.roll(centre[x][h], turn, 0)) for h in range(blocks_z)])
        fresh = []
        for x in range(rows_x):
            up_x, down_x = (x + 1) % rows_x, (x - 1) % rows_x
            front, back = ahead(centre[x], lane), behind(centre[x], lane)
            line = []
            for h in range(blocks_z):
                total = coef[0, x, h] * centre[x][h]
                total = total - coef[1, x, h] * centre[up_x][h]
                total = total - coef[1, down_x, h] * centre[down_x][h]
                total = total - coef[2, x, h] * inner[x][h]
                total = total - coef[3, x, h] * w[x][h]
                total = total - coef[4, x, h] * front[h]
                total = total - coef[5, x, h] * back[h]
                line.append(0.5 * total if step == 0 else total - last[x][h])
            fresh.append(line)
        last, w = inner, fresh
    return w


def edge_kernel(start, odd_ref, halo_ref, coef_ref, seam_ref, edge_ref):
    pairs, rows_x, blocks_z = edge_ref.shape[:3]
    row, lane = iotas()
    side = odd_ref[0]
    mark = row % DEGREE == jnp.where(side == 0, DEGREE - 1, 0)
    for pair in range(pairs):
        w = [[halo_ref[start + pair, x, :, cut(h)] for h in range(blocks_z)] for x in range(rows_x)]
        w = run_side(side, pair, w, seam_ref, coef_ref, lane, mark)
        for x in range(rows_x):
            for h in range(blocks_z):
                edge_ref[pair, x, h] = w[x][h]


def merge(first, second, place, odd, upper, edge_ref):
    for x in range(len(first)):
        for h in range(len(first[x])):
            a, b = first[x][h], second[x][h]
            top, bottom = jnp.where(odd, a, b), jnp.where(odd, b, a)
            edge_ref[place, x, h] = jnp.where(upper, top, pltpu.roll(bottom, DEGREE, 0))
            edge_ref[place + 1, x, h] = jnp.where(upper, pltpu.roll(top, DEGREE, 0), bottom)


def finish_kernel(start, odd_ref, halo_ref, coef_ref, seam_ref, sums_ref, second_ref, edge_ref, gram_ref):
    members, rows_x, blocks_z = edge_ref.shape[:3]
    row, lane = iotas()
    upper = row < DEGREE
    odd, side = odd_ref[0] == 1, 1 - odd_ref[0]
    mark = row % DEGREE == jnp.where(side == 0, DEGREE - 1, 0)
    for pair in range(members // 2):
        w = [[halo_ref[start + pair, x, :, cut(h)] for h in range(blocks_z)] for x in range(rows_x)]
        w = run_side(side, pair, w, seam_ref, coef_ref, lane, mark)
        second = [[second_ref[pair, x, h] for h in range(blocks_z)] for x in range(rows_x)]
        merge(w, second, 2 * pair, odd, upper, edge_ref)
    pairs = pairs_of(members)
    sums = [sums_ref[i] for i in range(len(pairs))]
    for x in range(rows_x):
        for h in range(blocks_z):
            f = [edge_ref[a, x, h] for a in range(members)]
            for i, (a, b) in enumerate(pairs):
                sums[i] = sums[i] + f[a] * f[b]
    at = {pair: jnp.sum(s, axis=0, keepdims=True) for pair, s in zip(pairs, sums)}
    column_of = lax.broadcasted_iota(jnp.int32, (members, members), 1)
    gram = jnp.zeros((members, members), jnp.float32)
    for a in range(members):
        column = jnp.concatenate([at[min(a, b), max(a, b)] for b in range(members)], 0)
        gram = jnp.where(column_of == a, jnp.sum(column, axis=1, keepdims=True), gram)
    gram_ref[...] = gram


def assemble_kernel(*refs):
    out_ref = refs[-1]
    rows_x, rows_y, depth = out_ref.shape[1:]
    row, _ = iotas()
    upper = row < DEGREE
    i = 0
    for body_ref, edge_ref in zip(refs[:-1:2], refs[1:-1:2]):
        for a in range(edge_ref.shape[0]):
            for x in range(rows_x):
                for h in range(depth // LANES):
                    body, edge = body_ref[a, x, h], edge_ref[a, x, h]
                    out_ref[i, x, 0:SUB, cut(h)] = jnp.where(upper, edge, body)
                    out_ref[i, x, rows_y - SUB :, cut(h)] = jnp.where(upper, body, edge)
            i += 1


def density_kernel(gram_ref, occ_ref, *refs):
    body_refs, edge_refs, out_ref = refs[:-1:2], refs[1:-1:2], refs[-1]
    rows_x, rows_y, depth = out_ref.shape
    blocks, members, _ = gram_ref.shape
    row, _ = iotas()
    upper = row < DEGREE
    down = lax.broadcasted_iota(jnp.int32, (members, members), 0)
    along = lax.broadcasted_iota(jnp.int32, (members, members), 1)
    w = []
    for k in range(blocks):
        ratio = jnp.broadcast_to(occ_ref[k : k + 1, :], (members, members)) / (gram_ref[k] + EPSILON)
        column = jnp.sum(jnp.where(down == along, ratio, 0.0), axis=1, keepdims=True)
        w += [jnp.broadcast_to(column[a : a + 1, :], (SUB, LANES)) for a in range(members)]
    for x in range(rows_x):
        for h in range(depth // LANES):
            body = edge = None
            for i in range(blocks * members):
                k, a = divmod(i, members)
                f, g = body_refs[k][a, x, h], edge_refs[k][a, x, h]
                f, g = w[i] * (f * f), w[i] * (g * g)
                body, edge = (f, g) if body is None else (body + f, edge + g)
            out_ref[x, 0:SUB, cut(h)] = jnp.where(upper, edge, body)
            out_ref[x, rows_y - SUB :, cut(h)] = jnp.where(upper, body, edge)


def vmem():
    return pl.BlockSpec(memory_space=pltpu.VMEM)


def smem():
    return pl.BlockSpec(memory_space=pltpu.SMEM)


def anywhere():
    return pl.BlockSpec(memory_space=pltpu.HBM)


def call(kernel, operands, outs, scratch=(), specs=None, place=jax.ShapeDtypeStruct, limit=8):
    shapes = tuple(place(shape, jnp.float32) for shape in outs)
    return pl.pallas_call(
        kernel,
        out_shape=shapes,
        in_specs=[vmem() for _ in operands] if specs is None else specs,
        out_specs=tuple(vmem() for _ in outs),
        scratch_shapes=[pltpu.VMEM(shape, jnp.float32) if isinstance(shape, tuple) else shape for shape in scratch],
        compiler_params=pltpu.CompilerParams(vmem_limit_bytes=limit * 1024 * 1024),
    )(*operands)


def fast_body(orbitals, potential, kinetic, occupations):
    blocks, members, _, rows_x, rows_y, depth = orbitals.shape
    count = blocks * members
    domains = lax.axis_size("grid")
    position = lax.axis_index("grid")
    parts = rows_y // SUB
    blocks_z = depth // LANES
    tile = (SUB, LANES)
    band = lax.axis_index("band")
    bands = lax.axis_size("band")
    odd = lax.rem(position, 2).astype(jnp.int32).reshape(1)
    core = lax.rem(band, 2).astype(jnp.int32).reshape(1)

    pairs_a = [(i, i ^ 1) for i in range(domains)]
    pairs_b = [(i, (i + 1) % domains if i % 2 else (i - 1) % domains) for i in range(domains)]
    half = members // 2
    whole = pltpu.with_memory_space_constraint(orbitals.reshape(count, rows_x, rows_y, depth), pltpu.HBM)
    block_shape = (members, rows_x, rows_y, depth)
    packed_a, packed_b, pot, kin, field = call(
        pack_kernel,
        (
            odd,
            core,
            pltpu.with_memory_space_constraint(potential[0], pltpu.HBM),
            pltpu.with_memory_space_constraint(kinetic[:, 0], pltpu.HBM),
            whole,
        ),
        [
            (2 + half, rows_x, SUB, depth),
            (1 + half, rows_x, SUB, depth),
            (rows_x, rows_y, depth),
            (3, rows_x, rows_y, depth),
            block_shape,
        ],
        [pltpu.SemaphoreType.DMA((3,))],
        specs=[smem()] * 2 + [anywhere()] * 3,
        place=pltpu.VMEM,
    )
    packs_a, packs_b, fields = [packed_a], [packed_b], [field]
    for k in range(1, blocks):
        packed_a, packed_b, field = call(
            functools.partial(rest_kernel, k),
            (odd, whole),
            [(half, rows_x, SUB, depth)] * 2 + [block_shape],
            [pltpu.SemaphoreType.DMA((1,))],
            specs=[smem(), anywhere()],
            place=pltpu.VMEM,
        )
        packs_a.append(packed_a)
        packs_b.append(packed_b)
        fields.append(field)
    halos = packs_a + packs_b
    halos_a = []
    for k in range(blocks):
        halos_a.append(lax.ppermute(halos[k], "grid", pairs_a))
    halos_b = []
    for k in range(blocks):
        halos_b.append(lax.ppermute(halos[blocks + k], "grid", pairs_b))
    other = swapped(halos_b[0][:1], "band", 1)

    inner = [
        call(
            interior_kernel,
            (pot, kin, fields[k]),
            [
                (members, rows_x, blocks_z) + tile,
                (2, half, DEGREE, 2, rows_x, blocks_z) + tile,
                (len(pairs_of(members)),) + tile,
            ],
            [
                (6, rows_x, parts, blocks_z) + tile,
                (4, rows_x, blocks_z, rows_y, LANES),
                (2, rows_x, blocks_z, rows_y, LANES),
            ],
        )
        for k in range(blocks)
    ]
    coef_shape = (DEGREE, 6, rows_x, blocks_z) + tile
    (coef_a,) = call(
        functools.partial(windows_kernel, 0),
        (odd, core, pot, kin, halos_a[0]),
        [coef_shape],
        specs=[smem()] * 2 + [vmem()] * 3,
    )
    (coef_b,) = call(
        functools.partial(windows_kernel, 1),
        (odd, core, pot, kin, halos_b[0], other),
        [coef_shape],
        specs=[smem()] * 2 + [vmem()] * 4,
    )
    rows, grams = [], []
    for k in range(blocks):
        body, seam, sums = inner[k]
        (second,) = call(
            functools.partial(edge_kernel, 0 if k else 1),
            (odd, halos_b[k], coef_b, seam),
            [(half, rows_x, blocks_z) + tile],
            specs=[smem()] + [vmem()] * 3,
        )
        edge, gram = call(
            functools.partial(finish_kernel, 0 if k else 2),
            (odd, halos_a[k], coef_a, seam, sums, second),
            [(members, rows_x, blocks_z) + tile, (members, members)],
            specs=[smem()] + [vmem()] * 5,
        )
        rows += [body, edge]
        grams.append(gram)
    gram = jnp.stack(grams)

    cells = rows_x * rows_y * depth * domains
    gram = gram * (1.0 / cells)
    bit = 1
    while bit < domains:
        gram = gram + swapped(gram, "grid", bit)
        bit *= 2

    (filtered,) = call(assemble_kernel, rows, [(count, rows_x, rows_y, depth)])
    (partial_value,) = call(density_kernel, (gram, occupations, *rows), [pot.shape])

    share = rows_y // bands
    value = partial_value.reshape(rows_x, bands, share, depth)
    bit = 1
    width = bands
    while bit < bands:
        value = value.reshape(rows_x, width // 2, 2, share, depth)
        mine = (band // bit) % 2
        keep = lax.dynamic_index_in_dim(value, mine, 2, False)
        send = lax.dynamic_index_in_dim(value, 1 - mine, 2, False)
        value = keep + swapped(send, "band", bit)
        bit *= 2
        width //= 2
    density = value.reshape(1, rows_x, share, depth)
    return filtered.reshape(orbitals.shape), gram, density


def extend(field, width, across):
    lower = shifted(field[..., -width:, :, :], "grid", across)
    upper = shifted(field[..., :width, :, :], "grid", -across)
    widened = jnp.concatenate([lower, field, upper], -3)
    column = lax.axis_index("grid") % across
    left_plain = shifted(widened[..., :, -width:, :], "grid", 1)
    left_wrap = shifted(widened[..., :, -width:, :], "grid", -(across - 1))
    left = jnp.where(column == 0, left_wrap, left_plain)
    right_plain = shifted(widened[..., :, :width, :], "grid", -1)
    right_wrap = shifted(widened[..., :, :width, :], "grid", across - 1)
    right = jnp.where(column == across - 1, right_wrap, right_plain)
    return jnp.concatenate([left, widened, right], -2)


def hamilton(field, coeffs):
    inner = field[..., 1:-1, 1:-1, :]
    kin_x = coeffs[1]
    total = kin_x[1:-1, 1:-1] * (inner - field[..., 2:, 1:-1, :])
    total = total + kin_x[:-2, 1:-1] * (inner - field[..., :-2, 1:-1, :])
    kin_y = coeffs[2]
    total = total + kin_y[1:-1, 1:-1] * (inner - field[..., 1:-1, 2:, :])
    total = total + kin_y[1:-1, :-2] * (inner - field[..., 1:-1, :-2, :])
    kin_z = coeffs[3, 1:-1, 1:-1]
    total = total + kin_z * (inner - jnp.roll(inner, -1, -1))
    total = total + jnp.roll(kin_z, 1, -1) * (inner - jnp.roll(inner, 1, -1))
    return 0.5 * total + coeffs[0, 1:-1, 1:-1] * inner


def general_body(across, orbitals, potential, kinetic, occupations):
    blocks = orbitals.shape[0]
    members = orbitals.shape[1]
    rows_x = orbitals.shape[3]
    rows_y = orbitals.shape[4]
    coeffs = jnp.concatenate([potential, kinetic[:, 0]], 0)
    current = orbitals[:, :, 0]
    previous = current
    coeff_ext = None
    for degree_step in range(DEGREE):
        if degree_step == 0:
            stacked = jnp.concatenate(
                [coeffs, current.reshape((blocks * members,) + current.shape[2:])], 0
            )
            wide = extend(stacked, 1, across)
            coeff_ext = wide[:4]
            extended = wide[4:].reshape((blocks, members) + wide.shape[1:])
        else:
            extended = extend(current, 1, across)
        image = hamilton(extended, coeff_ext)
        inner = extended[..., 1:-1, 1:-1, :]
        if degree_step == 0:
            fresh = (image - CENTRE * inner) / HALF_WIDTH
        else:
            fresh = 2.0 / HALF_WIDTH * (image - CENTRE * inner) - previous
        previous = current
        current = fresh
    cells = rows_x * rows_y * orbitals.shape[5] * lax.axis_size("grid")
    flat = current.reshape(blocks, members, -1)
    local_gram = jnp.einsum("kbx,kcx->kbc", flat, flat, precision=lax.Precision.HIGHEST) / cells
    gram = lax.psum(local_gram, "grid")
    diagonal = jnp.diagonal(gram, axis1=1, axis2=2)
    weight = occupations / (diagonal + EPSILON)
    partial_value = jnp.einsum(
        "kb,kbxyz->xyz", weight, current * current, precision=lax.Precision.HIGHEST
    )
    density = lax.psum_scatter(partial_value[None], "band", scatter_dimension=2, tiled=True)
    return (current[:, :, None], gram, density)


def solution(mesh):
    domains = mesh.shape["grid"]
    across = min(domains, 8)
    even = all(size > 1 and size & (size - 1) == 0 for size in mesh.shape.values())
    fast = domains == across and even
    whole = fast_body if fast else functools.partial(general_body, across)

    placed = (
        P("band", None, "grid", None, None, None),
        P("grid", None, None, None),
        P(None, "grid", None, None, None),
        P("band", None),
    )
    return jax.shard_map(
        whole,
        mesh=mesh,
        in_specs=placed,
        out_specs=(
            P("band", None, "grid", None, None, None),
            P("band", None, None),
            P("grid", None, "band", None),
        ),
        check_vma=False,
    )
```
